256 devices in a mesh: user: 32 (over x_lo, z, core), tensor: 8 (over y, x_hi).
Axes of the slice: x: 4 (x_hi: 2, x_lo: 2; x = x_hi * 2 + x_lo), y: 4, z: 8, core: 2. Of those that a mesh axis runs over, the one named last changes fastest.
Arguments:
- events: bfloat16 [1024, 128, 1024], P('user', None, 'tensor'), may hold values from -6 to 6
- cotangent: bfloat16 [1024, 128, 1024], P('user', None, 'tensor'), may hold values from -6 to 6
- w_in: bfloat16 [1024, 4096], P('user', 'tensor'), may hold values from -0.1875 to 0.1875
- w_out: bfloat16 [1024, 1024], P('user', 'tensor'), may hold values from -0.1875 to 0.1875
- slot_source: int32 [1024], P('user'), may hold values from 0 to 31, as said below
- slot_length: int32 [1024], P('user'), may hold values from 1 to 127, as said below
Outputs:
- grad_x: bfloat16 [1024, 128, 1024], P('user', None, 'tensor')
- grad_w_in: float32 [1024, 4096], P('user', 'tensor')
- grad_w_out: float32 [1024, 1024], P('user', 'tensor')
The draws below stay inside these ranges and needn't reach their ends.
Inputs may be any that keep to these rules, and one draw needn't show every extreme that they name: `slot_source`: the 32 slots of one host name distinct user shards, and for each slot j the entries h * 32 + j over all hosts h name every user shard once, so every history is placed exactly once. `slot_length`: the 32 slot lengths of one host sum to 2048.
All inputs are finite; a program needn't handle non-finite values.
Results may differ from the reference program's by a relative error of at most 0.023.
Values may be sent and summed in bfloat16 or wider, within the bound.
A program may use at most 128 MiB of HBM per device.

```python
import jax
import jax.numpy as jnp
from jax import lax

D = 1024
HEADS = 8
HEAD_DIM = 128
SEQ_LEN = 128
HIST_DEV = 32
ROWS = 2048
NSEQ = 1024
N_USER = 32


def placement_tables(key):
    base = jax.random.fold_in(key, 7)
    key_p, key_t, key_c, key_l, key_s = jax.random.split(base, 5)
    count = N_USER
    first = jax.random.permutation(key_p, count).astype(jnp.int32)
    second = jax.random.permutation(key_t, count).astype(jnp.int32)
    offsets = jax.random.permutation(key_c, count).astype(jnp.int32)[:HIST_DEV]
    owners = jnp.arange(count, dtype=jnp.int32)[:, None]
    second_inv = jnp.argsort(second, stable=True).astype(jnp.int32)
    first_inv = jnp.argsort(first, stable=True).astype(jnp.int32)
    sources = first_inv[(second_inv[owners] - offsets[None, :]) % count]
    halves = jax.random.randint(key_l, (count, HIST_DEV // 2), 1, SEQ_LEN).astype(jnp.int32)
    halves = halves.at[:, 0].set(SEQ_LEN - 1)
    pairs = jnp.stack([halves, SEQ_LEN - halves], axis=-1).reshape(count, HIST_DEV)
    scores = jax.random.randint(key_s, (count, HIST_DEV), 0, 1 << 20) * HIST_DEV + jnp.arange(HIST_DEV, dtype=jnp.int32)[None, :]
    order = jnp.argsort(scores, axis=1, stable=True)
    lengths = jnp.take_along_axis(pairs, order, axis=1)
    return (sources.reshape(-1).astype(jnp.int32), lengths.reshape(-1).astype(jnp.int32))


def draw_slot_source(key, part):
    return placement_tables(key)[0]


def draw_slot_length(key, part):
    return placement_tables(key)[1]


def raised(drawn, own_key, source, target, shards_of, factor):
    owner, partner = [(jnp.arange(drawn.shape[dim]) // (drawn.shape[dim] // shards_of)).reshape([-1 if axis == dim else 1 for axis in range(drawn.ndim)]) for dim in (source, target)]
    chosen = jax.random.permutation(own_key, shards_of)[partner]
    strong = (owner == chosen) | (owner == (partner + shards_of // 2) % shards_of)
    return jnp.where(strong, factor * drawn, drawn)


def steps_of(key, dims, pieces, low, top_value):
    def one(dim, blocks):
        heights = jax.random.uniform(jax.random.fold_in(jax.random.fold_in(key, 6), dim), (blocks,), jnp.float32, low / len(pieces), top_value / len(pieces))
        return jnp.repeat(jnp.exp(heights), dims[dim] // blocks).reshape((-1,) + (1,) * (len(dims) - dim - 1))

    factor_of = one(*pieces[0])
    for cut in pieces[1:]:
        factor_of = factor_of * one(*cut)
    return factor_of


def noise(own_key, shape, spread, limit, cuts=(), kind=jnp.bfloat16):
    loudness = steps_of(own_key, shape, cuts, -0.22, 0.18) if cuts else 1.0
    array = jax.random.normal(own_key, shape, jnp.float32) * spread * loudness
    return jnp.minimum(jnp.maximum(array, -limit), limit).astype(kind)


def heavy_noise(rng, shape, scale, reach, cuts, heavy, kind=jnp.bfloat16):
    array = scale * jax.random.normal(rng, shape, jnp.float32)
    if cuts:
        array = array * steps_of(rng, shape, cuts, -0.22, 0.18)
    return jnp.clip(raised(array, jax.random.fold_in(rng, 3), *heavy), -reach, reach).astype(kind)


def setup_inputs(seed: int = 0) -> dict:
    key_of = jax.random.split(jax.random.key(seed), 7)
    return {
        "events": noise(key_of[0], (NSEQ, SEQ_LEN, D), 1.0, 6.0, ((0, 32), (2, 8))),
        "cotangent": heavy_noise(key_of[1], (NSEQ, SEQ_LEN, D), 1.0, 6.0, ((0, 32), (2, 8)), (0, 2, 32, 2.75)),
        "w_in": noise(key_of[2], (D, 4 * D), D ** -0.5, 0.1875, ((0, 32), (1, 8))),
        "w_out": noise(key_of[3], (D, D), D ** -0.5, 0.1875, ((0, 32), (1, 8))),
        "slot_source": draw_slot_source(jax.random.fold_in(key_of[6], 71), 0),
        "slot_length": draw_slot_length(jax.random.fold_in(key_of[6], 71), 0),
    }


eps = 1e-05

def silu_grad(t):
    sig = jax.nn.sigmoid(t)
    return sig * (1.0 + t * (1.0 - sig))

def host_rows(lengths, sources):
    ends = jnp.cumsum(lengths).astype(jnp.int32)
    starts = (ends - lengths).astype(jnp.int32)
    rows = jnp.arange(ROWS, dtype=jnp.int32)
    segment = lax.optimization_barrier(jnp.sum((rows[:, None] >= ends[None, :]).astype(jnp.int32), axis=1)).astype(jnp.int32)
    onehot = (segment[:, None] == jnp.arange(HIST_DEV, dtype=jnp.int32)[None, :]).astype(jnp.int32)
    position = (rows - lax.optimization_barrier(jnp.sum(onehot * starts[None, :], axis=1))).astype(jnp.int32)
    source = lax.optimization_barrier(jnp.sum(onehot * sources[None, :], axis=1)).astype(jnp.int32)
    return (segment, position, source)

def host_pass(x_flat, d_flat, w_in, w_out, lengths, sources):
    segment, position, source = host_rows(lengths, sources)
    index = ((source * HIST_DEV + segment) * SEQ_LEN + position).astype(jnp.int32)
    xp = jnp.take(x_flat, index, axis=0)
    dp = jnp.take(d_flat, index, axis=0)
    xf = xp.astype(jnp.float32)
    centred = xf - lax.optimization_barrier(jnp.mean(xf, axis=1, keepdims=True))
    rstd = lax.rsqrt(lax.optimization_barrier(jnp.mean(centred * centred, axis=1, keepdims=True)) + eps)
    nf = centred * rstd
    nb = nf.astype(jnp.bfloat16)
    z = jnp.dot(nb, w_in, preferred_element_type=jnp.float32)
    g = jax.nn.silu(z).astype(jnp.bfloat16).reshape(ROWS, HEADS, 4, HEAD_DIM)
    mask = (segment[:, None] == segment[None, :]) & (position[None, :] <= position[:, None])
    dh = jnp.dot(dp, w_out, preferred_element_type=jnp.float32).reshape(ROWS, HEADS, HEAD_DIM)
    scale = HEAD_DIM ** (-0.5)

    def one_head(items):
        parts, grad_h = items
        upart, vpart, qpart, kpart = (parts[:, 0], parts[:, 1], parts[:, 2], parts[:, 3])
        scores = jnp.dot(qpart, kpart.T, preferred_element_type=jnp.float32) * scale
        attn = jnp.where(mask, jax.nn.silu(scores) / SEQ_LEN, 0.0).astype(jnp.bfloat16)
        yval = jnp.dot(attn, vpart, preferred_element_type=jnp.float32)
        ycen = yval - lax.optimization_barrier(jnp.mean(yval, axis=1, keepdims=True))
        yrstd = lax.rsqrt(lax.optimization_barrier(jnp.mean(ycen * ycen, axis=1, keepdims=True)) + eps)
        ynorm = ycen * yrstd
        uf = upart.astype(jnp.float32)
        hpart = (ynorm * uf).astype(jnp.bfloat16)
        grad_u = grad_h * ynorm
        grad_yn = grad_h * uf
        grad_y = ((grad_yn - lax.optimization_barrier(jnp.mean(grad_yn, axis=1, keepdims=True)) - ynorm * lax.optimization_barrier(jnp.mean(grad_yn * ynorm, axis=1, keepdims=True))) * yrstd).astype(jnp.bfloat16)
        grad_a = jnp.dot(grad_y, vpart.T, preferred_element_type=jnp.float32)
        grad_v = jnp.dot(attn.T, grad_y, preferred_element_type=jnp.float32)
        grad_s = jnp.where(mask, grad_a * silu_grad(scores) * (scale / SEQ_LEN), 0.0).astype(jnp.bfloat16)
        grad_q = jnp.dot(grad_s, kpart, preferred_element_type=jnp.float32)
        grad_k = jnp.dot(grad_s.T, qpart, preferred_element_type=jnp.float32)
        return (hpart, jnp.stack([grad_u, grad_v, grad_q, grad_k], axis=1))
    hparts, grads = lax.map(one_head, (g.transpose(1, 0, 2, 3), dh.transpose(1, 0, 2)))
    hb = hparts.transpose(1, 0, 2).reshape(ROWS, D)
    dgrad = grads.transpose(1, 0, 2, 3).reshape(ROWS, 4 * D)
    dz = (dgrad * silu_grad(z)).astype(jnp.bfloat16)
    grad_in = jnp.dot(nb.T, dz, preferred_element_type=jnp.float32)
    grad_out = jnp.dot(dp.T, hb, preferred_element_type=jnp.float32)
    dn = jnp.dot(dz, w_in.T, preferred_element_type=jnp.float32)
    branch = (dn - lax.optimization_barrier(jnp.mean(dn, axis=1, keepdims=True)) - nf * lax.optimization_barrier(jnp.mean(dn * nf, axis=1, keepdims=True))) * rstd
    dxp = (dp.astype(jnp.float32) + branch).astype(jnp.bfloat16)
    return (dxp, grad_in, grad_out, index)

def reference(events, cotangent, w_in, w_out, slot_source, slot_length):
    x_flat = events.reshape(NSEQ * SEQ_LEN, D)
    d_flat = cotangent.reshape(NSEQ * SEQ_LEN, D)
    sources = slot_source.reshape(N_USER, HIST_DEV)
    lengths = slot_length.reshape(N_USER, HIST_DEV)

    def step(carry, item):
        acc_in, acc_out = carry
        dxp, grad_in, grad_out, index = host_pass(x_flat, d_flat, w_in, w_out, item[0], item[1])
        return ((acc_in + grad_in, acc_out + grad_out), (dxp, index))
    start = (jnp.zeros((D, 4 * D), jnp.float32), jnp.zeros((D, D), jnp.float32))
    (grad_w_in, grad_w_out), (dxs, indices) = lax.scan(step, start, (lengths, sources))
    grad_x = jnp.zeros((NSEQ * SEQ_LEN, D), jnp.bfloat16).at[indices.reshape(-1)].set(dxs.reshape(-1, D))
    return (grad_x.reshape(NSEQ, SEQ_LEN, D), grad_w_in, grad_w_out)
```

```python
import functools

import jax
import jax.numpy as jnp
from jax import lax
from jax.experimental import pallas as pl
from jax.experimental.pallas import tpu as pltpu
from jax.sharding import PartitionSpec as P

MESH = pl.DeviceIdType.MESH
F32 = jnp.float32
BF16 = jnp.bfloat16
EPS = 1e-05
HD = 128
SEQ = 128
HEADS = 8
NX, NY, NZ = 4, 4, 8
HIST = 4
ROWS = HIST * SEQ
D = 1024

COLOURS = ((2, NZ, NX * NY, 384), (0, NX, NY * NZ, 128), (1, NY, NX * NZ, 128))


def place():
    u = lax.axis_index("user")
    t = lax.axis_index("tensor")
    c = lax.rem(u, 2)
    z = lax.rem(u // 2, NZ)
    x = lax.rem(t, 2) * 2 + u // (2 * NZ)
    y = t // 2
    return u, t, c, (x, y, z)


def device_of(x, y, z, c):
    return ((lax.rem(x, 2) * NZ + z) * 2 + c, y * 2 + x // 2)


def ring_and_plane(colour, pos):
    x, y, z = pos
    return ((z, y * NX + x), (x, y * NZ + z), (y, x * NZ + z))[colour]


def plane_device(colour, pos, p, c):
    x, y, z = pos
    if colour == 0:
        return device_of(lax.rem(p, NX), p // NX, z, c)
    if colour == 1:
        return device_of(x, p // NZ, lax.rem(p, NZ), c)
    return device_of(p // NZ, y, lax.rem(p, NZ), c)


def ring_device(colour, pos, step, c):
    axis, n = COLOURS[colour][:2]
    pos = list(pos)
    pos[axis] = lax.rem(pos[axis] + step + n, n)
    return device_of(*pos, c)


def remote(src, dst, send, recv, device):
    return pltpu.make_async_remote_copy(
        src_ref=src, dst_ref=dst, send_sem=send, recv_sem=recv, device_id=device, device_id_type=MESH
    )


def wait_bytes(ref, sem):
    pltpu.make_async_copy(ref, ref, sem).wait()


def gather_kernel(
    ev, ct, w_in, w_out, tab, gz, gx, gy, xr, dr, tabs,
    bounce, plane_send, plane_recv, rs, rr, fwd_send, fwd_recv, a2a_send, a2a_recv, tab_send, tab_recv, loc,
):
    u, t, c, pos = place()
    gs = (gz, gx, gy)
    pieces = (w_in.at[:, pl.ds(0, 384)], w_in.at[:, pl.ds(384, 128)], w_out)
    partner = (u + 1 - 2 * c, t)
    locals_ = []

    for col in (1, 2, 0):
        n, m = COLOURS[col][1:3]
        a, p = ring_and_plane(col, pos)
        own = pltpu.make_async_copy(pieces[col], gs[col].at[c, a, p], loc.at[col])
        own.start()
        locals_.append(own)

        @pl.loop(1, m)
        def _(i):
            q = lax.rem(p + i, m)
            remote(
                pieces[col], gs[col].at[c, a, p], plane_send.at[col], plane_recv.at[col],
                plane_device(col, pos, q, c),
            ).start()

    @pl.loop(1, HEADS)
    def _(i):
        q = lax.rem(t + i, HEADS)
        for k, (src, dst) in enumerate(((ev, xr), (ct, dr))):
            remote(src.at[pl.ds(q * HIST, HIST)], dst.at[t], a2a_send.at[k], a2a_recv.at[k], (u, q)).start()

    ins = []
    for k, src in enumerate((ev, ct)):
        copy = pltpu.make_async_copy(src.at[pl.ds(t * HIST, HIST)], bounce.at[k], loc.at[3 + k])
        copy.start()
        ins.append(copy)

    @pl.loop(1, 32)
    def _(i):
        remote(tab, tabs.at[u], tab_send, tab_recv, (lax.rem(u + i, 32), t)).start()

    own_tab = pltpu.make_async_copy(tab, tabs.at[u], loc.at[5])
    own_tab.start()
    for k, dst in enumerate((xr, dr)):
        ins[k].wait()
        copy = pltpu.make_async_copy(bounce.at[k], dst.at[t], loc.at[6 + k])
        copy.start()
        locals_.append(copy)
    locals_.append(own_tab)
    for copy in locals_:
        copy.wait()

    sends = []

    def sem_index(col, direction, k, half):
        base = (0, 16, 24)[col]
        return base + (direction * (COLOURS[col][1] // 2) + k) * 2 + half

    def halves(col, k, direction):
        if k == COLOURS[col][1] // 2 - 1:
            return (direction,)
        return (0, 1)

    def block(col, idx, half):
        m = COLOURS[col][2]
        return gs[col].at[c, idx, pl.ds(half * (m // 2), m // 2)]

    def forward(col, idx, half):
        part = block(col, idx, half)
        remote(part, part, fwd_send.at[col], fwd_recv.at[col], partner).start()

    def ring_send(col, k, direction, half):
        n = COLOURS[col][1]
        a, _ = ring_and_plane(col, pos)
        step = 1 - 2 * direction
        part = block(col, lax.rem(a - step * k + n, n), half)
        s = sem_index(col, direction, k, half)
        copy = remote(part, part, rs.at[s], rr.at[s], ring_device(col, pos, step, c))
        copy.start()
        sends.append(copy)

    def ring_wait(col, k, direction, half):
        n = COLOURS[col][1]
        a, _ = ring_and_plane(col, pos)
        step = 1 - 2 * direction
        idx = lax.rem(a - step * (k + 1) + n, n)
        s = sem_index(col, direction, k, half)
        wait_bytes(block(col, idx, half), rr.at[s])
        forward(col, idx, half)

    for col in (1, 2, 0):
        m = COLOURS[col][2]
        a, p = ring_and_plane(col, pos)
        wait_bytes(gs[col].at[c, a, pl.ds(0, m - 1)], plane_recv.at[col])
        for half in (0, 1):
            for direction in (0, 1):
                if half in halves(col, 0, direction):
                    ring_send(col, 0, direction, half)
        for half in (0, 1):
            forward(col, a, half)

    for k in range(NZ // 2):
        for col in (1, 2, 0):
            if k >= COLOURS[col][1] // 2:
                continue
            for half in (0, 1):
                for direction in (0, 1):
                    if half in halves(col, k, direction):
                        ring_wait(col, k, direction, half)
                        if k + 1 < COLOURS[col][1] // 2 and half in halves(col, k + 1, direction):
                            ring_send(col, k + 1, direction, half)

    for copy in sends:
        copy.wait_send()
    for col in range(3):
        m = COLOURS[col][2]
        a, p = ring_and_plane(col, pos)
        wait_bytes(gs[col].at[c, a, pl.ds(0, m - 1)], plane_send.at[col])
        wait_bytes(gs[col].at[c], fwd_send.at[col])
        wait_bytes(gs[col].at[1 - c], fwd_recv.at[col])
    for k, ref in enumerate((xr, dr)):
        wait_bytes(ref.at[pl.ds(0, HEADS - 1)], a2a_send.at[k])
        wait_bytes(ref.at[pl.ds(0, HEADS - 1)], a2a_recv.at[k])
    wait_bytes(tabs.at[pl.ds(0, 31)], tab_send)
    wait_bytes(tabs.at[pl.ds(0, 31)], tab_recv)


def gather(events, cotangent, w_in, w_out, tab):
    any_ = pl.BlockSpec(memory_space=pl.ANY)
    vmem = pl.BlockSpec(memory_space=pltpu.VMEM)
    shape = jax.ShapeDtypeStruct
    out_shape = tuple(shape((2, n, m, 32, w), BF16) for _, n, m, w in COLOURS) + (
        shape((HEADS, HIST, SEQ, 128), BF16),
        shape((HEADS, HIST, SEQ, 128), BF16),
        shape((32, 8, 128), jnp.int32),
    )
    dma = pltpu.SemaphoreType.DMA
    return pl.pallas_call(
        gather_kernel,
        out_shape=out_shape,
        in_specs=[any_, any_, vmem, vmem, any_],
        out_specs=(any_,) * 6,
        scratch_shapes=[
            pltpu.VMEM((2, HIST, SEQ, 128), BF16),
            dma((3,)), dma((3,)), dma((32,)), dma((32,)), dma((3,)), dma((3,)),
            dma((2,)), dma((2,)), dma, dma, dma((8,)),
        ],
        compiler_params=pltpu.CompilerParams(has_side_effects=True),
        name="gather",
    )(events, cotangent, w_in, w_out, tab)


def silu_parts(v):
    sig = jax.nn.sigmoid(v)
    return v * sig, sig * (1.0 + v * (1.0 - sig))


def dot(a, b, dims):
    return lax.dot_general(a, b, (dims, ((), ())), preferred_element_type=F32)


NN, NT, TN = ((1,), (0,)), ((1,), (1,)), ((0,), (0,))


def layer_kernel(
    xr, dr, tabs, gz, gx, gy, pz, px, py, dxr,
    nf, nb, nbt, dm, dmt, rstd_s, dn, wh, wo, dz_s, hb_s,
):
    h = pl.program_id(0)

    @pl.when(h == 0)
    def _():
        u = lax.axis_index("user")
        t = lax.axis_index("tensor")
        lens = jnp.sum(jnp.where(tabs[:, 0, :] == u, tabs[:, 1, :], 0).astype(F32), axis=0, keepdims=True)
        lane = lax.broadcasted_iota(jnp.int32, (1, 128), 1)
        for i in range(HIST):
            rows = pl.ds(i * SEQ, SEQ)
            xs = jnp.concatenate([xr[k, i] for k in range(HEADS)], axis=1).astype(F32)
            cen = xs - jnp.mean(xs, axis=1, keepdims=True)
            rstd = lax.rsqrt(jnp.mean(cen * cen, axis=1, keepdims=True) + EPS)
            nfi = cen * rstd
            nf[rows, :] = nfi
            rstd_s[rows, :] = jnp.broadcast_to(rstd, (SEQ, 128))
            nbi = nfi.astype(BF16)
            nb[rows, :] = nbi
            nbt[:, rows] = nbi.T
            length = jnp.sum(jnp.where(lane == t * HIST + i, lens, 0.0), axis=1, keepdims=True)
            pos = lax.broadcasted_iota(jnp.int32, (SEQ, D), 0).astype(F32)
            ds_ = jnp.concatenate([dr[k, i] for k in range(HEADS)], axis=1).astype(F32)
            di = jnp.where(pos < length, ds_, 0.0).astype(BF16)
            dm[rows, :] = di
            dmt[:, rows] = di.T
        dn[...] = jnp.zeros_like(dn)

    for xl in range(2):
        for z in range(NZ):
            for c in range(2):
                r = pl.ds(((xl * NZ + z) * 2 + c) * 32, 32)
                wh[r, pl.ds(0, 384)] = gz[c, z, 0, xl]
                wh[r, pl.ds(384, 128)] = gx[c, 0, xl, 0, z]
                wo[r, :] = gy[c, 0, xl, z]

    scale = HD ** (-0.5)
    causal = lax.broadcasted_iota(jnp.int32, (SEQ, SEQ), 1) <= lax.broadcasted_iota(jnp.int32, (SEQ, SEQ), 0)
    for i in range(HIST):
        rows = pl.ds(i * SEQ, SEQ)
        zi = dot(nb[rows, :], wh[...], NN)
        gi, sgi = silu_parts(zi)
        gi = gi.astype(BF16)
        grad_h = dot(dm[rows, :], wo[...], NN)
        uf = gi[:, 0:128].astype(F32)
        vp, qp, kp = gi[:, 128:256], gi[:, 256:384], gi[:, 384:512]
        s = dot(qp, kp, NT) * scale
        ss, sgs = silu_parts(s)
        at = jnp.where(causal, ss / SEQ, 0.0).astype(BF16)
        yv = dot(at, vp, NN)
        ycen = yv - jnp.mean(yv, axis=1, keepdims=True)
        yrstd = lax.rsqrt(jnp.mean(ycen * ycen, axis=1, keepdims=True) + EPS)
        yn = ycen * yrstd
        hb_s[rows, :] = (yn * uf).astype(BF16)
        grad_u = grad_h * yn
        gyn = grad_h * uf
        dy = (
            (gyn - jnp.mean(gyn, axis=1, keepdims=True) - yn * jnp.mean(gyn * yn, axis=1, keepdims=True)) * yrstd
        ).astype(BF16)
        da = dot(dy, vp, NT)
        grad_v = dot(at, dy, TN)
        ds_ = jnp.where(causal, da * sgs * (scale / SEQ), 0.0).astype(BF16)
        grad_q = dot(ds_, kp, NN)
        grad_k = dot(ds_, qp, TN)
        dz_s[rows, :] = (jnp.concatenate([grad_u, grad_v, grad_q, grad_k], axis=1) * sgi).astype(BF16)

    for j in range(4):
        gw = dot(nbt[pl.ds(j * 256, 256), :], dz_s[...], NN).astype(BF16)
        go = dot(dmt[pl.ds(j * 256, 256), :], hb_s[...], NN).astype(BF16)
        for k in range(8):
            uu = j * 8 + k
            c, z, xl = uu % 2, (uu // 2) % NZ, uu // (2 * NZ)
            pz[c, z, 0, xl] = gw[k * 32 : k * 32 + 32, 0:384]
            px[c, 0, xl, 0, z] = gw[k * 32 : k * 32 + 32, 384:512]
            py[c, 0, xl, z] = go[k * 32 : k * 32 + 32, :]
        dn[:, pl.ds(j * 256, 256)] += dot(dz_s[...], wh[pl.ds(j * 256, 256), :], NT)

    @pl.when(h == HEADS - 1)
    def _():
        for i in range(HIST):
            rows = pl.ds(i * SEQ, SEQ)
            dni, nfi = dn[rows, :], nf[rows, :]
            branch = (
                dni - jnp.mean(dni, axis=1, keepdims=True) - nfi * jnp.mean(dni * nfi, axis=1, keepdims=True)
            ) * rstd_s[rows, 0:1]
            out = (dm[rows, :].astype(F32) + branch).astype(BF16)
            for k in range(HEADS):
                dxr[k, i] = out[:, k * 128 : k * 128 + 128]


def layer(xr, dr, tabs, gz, gx, gy):
    full = lambda shape: pl.BlockSpec(shape, lambda h: (0,) * len(shape), pipeline_mode=pl.Buffered(1))
    zspec = pl.BlockSpec((2, NZ, 1, 2, 32, 384), lambda h: (0, 0, h, 0, 0, 0))
    xspec = pl.BlockSpec((2, 1, 2, 1, NZ, 32, 128), lambda h: (0, lax.rem(h, 2), 0, h // 2, 0, 0, 0))
    yspec = pl.BlockSpec((2, 1, 2, NZ, 32, 128), lambda h: (0, h, 0, 0, 0, 0))
    zs, xs, ys = (2, NZ, HEADS, 2, 32, 384), (2, 2, 2, NY, NZ, 32, 128), (2, HEADS, 2, NZ, 32, 128)
    shape = jax.ShapeDtypeStruct
    rows = (HEADS, HIST, SEQ, 128)
    pz, px, py, dxr = pl.pallas_call(
        layer_kernel,
        grid=(HEADS,),
        out_shape=(shape(zs, BF16), shape(xs, BF16), shape(ys, BF16), shape(rows, BF16)),
        in_specs=[full(rows), full(rows), full((32, 8, 128)), zspec, xspec, yspec],
        out_specs=(zspec, xspec, yspec, pl.BlockSpec(rows, lambda h: (0,) * 4)),
        scratch_shapes=[
            pltpu.VMEM((ROWS, D), F32),
            pltpu.VMEM((ROWS, D), BF16),
            pltpu.VMEM((D, ROWS), BF16),
            pltpu.VMEM((ROWS, D), BF16),
            pltpu.VMEM((D, ROWS), BF16),
            pltpu.VMEM((ROWS, 128), F32),
            pltpu.VMEM((ROWS, D), F32),
            pltpu.VMEM((D, 512), BF16),
            pltpu.VMEM((D, 128), BF16),
            pltpu.VMEM((ROWS, 512), BF16),
            pltpu.VMEM((ROWS, 128), BF16),
        ],
        compiler_params=pltpu.CompilerParams(
            dimension_semantics=("arbitrary",), vmem_limit_bytes=56 * 1024 * 1024
        ),
        name="layer",
    )(xr, dr, tabs, gz.reshape(zs), gx.reshape(xs), gy.reshape(ys))
    return [p.reshape((2, n, m, 32, w)) for p, (_, n, m, w) in zip((pz, px, py), COLOURS)] + [dxr]


def scatter_kernel(
    pz, px, py, dxr, grad_x, grad_wi, grad_wo,
    az, ax, ay, bz, bx, by, rz, rx, ry, qz, qx, qy, bounce,
    par_send, par_recv, ld, rs, rr, plane_send, plane_recv, a2a_send, a2a_recv, loc,
):
    u, t, c, pos = place()
    partner = (u + 1 - 2 * c, t)
    ps, accs, theirs, rings, planes = (pz, px, py), (az, ax, ay), (bz, bx, by), (rz, rx, ry), (qz, qx, qy)

    def block_sem(col, idx, half):
        return (0, 16, 24)[col] + idx * 2 + half

    def part(ref, col, idx, half):
        m = COLOURS[col][2]
        return ref.at[idx, pl.ds(half * (m // 2), m // 2)]

    def order(col, j):
        n = COLOURS[col][1]
        return (n // 2 - j, j - n // 2)

    def offsets(col):
        n = COLOURS[col][1]
        out = []
        for j in range(n // 2 + 1):
            for o in order(col, j):
                if o % n not in out:
                    out.append(o % n)
        return out

    def index(col, off):
        n = COLOURS[col][1]
        a, _ = ring_and_plane(col, pos)
        return lax.rem(a + off + n, n)

    def start_block(col, off):
        idx = index(col, off)
        m = COLOURS[col][2]
        for half in (0, 1):
            s = (0, 16, 24)[col] + (off % COLOURS[col][1]) * 2 + half
            sub = pl.ds(half * (m // 2), m // 2)
            remote(
                ps[col].at[1 - c, idx, sub], part(theirs[col], col, idx, half), par_send.at[s], par_recv.at[s], partner
            ).start()
            pltpu.make_async_copy(ps[col].at[c, idx, sub], part(accs[col], col, idx, half), ld.at[s]).start()

    for j in range(NZ // 2 + 1):
        for col in (0, 1, 2):
            n = COLOURS[col][1]
            if j > n // 2:
                continue
            offs = sorted({o % n for o in order(col, j)})
            for off in offs:
                start_block(col, off)

    ins = pltpu.make_async_copy(dxr.at[t], bounce, loc.at[0])
    ins.start()

    @pl.loop(1, HEADS)
    def _(i):
        q = lax.rem(t + i, HEADS)
        remote(dxr.at[q], grad_x.at[pl.ds(t * HIST, HIST)], a2a_send, a2a_recv, (u, q)).start()

    ins.wait()
    own = pltpu.make_async_copy(bounce, grad_x.at[pl.ds(t * HIST, HIST)], loc.at[1])
    own.start()

    def ring_slot(col, k, direction, half):
        n = COLOURS[col][1]
        return (direction * (n // 2) + k) * 2 + half

    sends = []

    def add(col, off, half, slots):
        idx = index(col, off)
        m = COLOURS[col][2]
        s = (0, 16, 24)[col] + (off % COLOURS[col][1]) * 2 + half
        mine = part(accs[col], col, idx, half)
        other = part(theirs[col], col, idx, half)
        wait_bytes(mine, ld.at[s])
        wait_bytes(other, par_recv.at[s])
        got = []
        for k, direction in slots:
            slot = ring_slot(col, k, direction, half)
            ref = rings[col].at[slot]
            wait_bytes(ref, rr.at[(0, 16, 24)[col] + slot])
            got.append(ref)

        @pl.loop(0, m // 2)
        def _(i):
            v = mine[i].astype(F32) + other[i].astype(F32)
            for ref in got:
                v = v + ref[i].astype(F32)
            mine[i] = v.astype(BF16)

    def ring_send(col, k, direction, half, off):
        idx = index(col, off)
        slot = ring_slot(col, k, direction, half)
        s = (0, 16, 24)[col] + slot
        copy = remote(
            part(accs[col], col, idx, half), rings[col].at[slot], rs.at[s], rr.at[s],
            ring_device(col, pos, 1 - 2 * direction, c),
        )
        copy.start()
        sends.append(copy)

    for k in range(NZ // 2):
        for col in (1, 2, 0):
            n = COLOURS[col][1]
            if k >= n // 2:
                continue
            for half in (0, 1):
                for direction in (0, 1):
                    off = order(col, k)[direction]
                    if k == 0:
                        if half == direction:
                            add(col, off, half, ())
                            ring_send(col, k, direction, half, off)
                        continue
                    slots = ((k - 1, direction),) if (k > 1 or half == direction) else ()
                    add(col, off, half, slots)
                    ring_send(col, k, direction, half, off)

    for col in (1, 2, 0):
        n, m, w = COLOURS[col][1:]
        a, p = ring_and_plane(col, pos)
        for half in (0, 1):
            k = n // 2 - 1
            slots = tuple((k, d) for d in (0, 1))
            add(col, 0, half, slots)

        @pl.loop(1, m)
        def _(i):
            q = lax.rem(p + i, m)
            remote(
                accs[col].at[a, q], planes[col].at[p], plane_send.at[col], plane_recv.at[col],
                plane_device(col, pos, q, c),
            ).start()

    outs = (grad_wi.at[:, pl.ds(0, 384)], grad_wi.at[:, pl.ds(384, 128)], grad_wo)
    for col in (1, 2, 0):
        n, m, w = COLOURS[col][1:]
        a, p = ring_and_plane(col, pos)
        wait_bytes(planes[col].at[pl.ds(0, m - 1)], plane_recv.at[col])
        mine = accs[col].at[a, p]

        def body(i, total):
            return total + planes[col][lax.rem(p + i, m)].astype(F32)

        outs[col][...] = lax.fori_loop(1, m, body, mine[...].astype(F32))

    for copy in sends:
        copy.wait_send()
    for col in range(3):
        n, m, w = COLOURS[col][1:]
        wait_bytes(planes[col].at[pl.ds(0, m - 1)], plane_send.at[col])
        for off in range(n):
            for half in (0, 1):
                s = (0, 16, 24)[col] + off * 2 + half
                wait_bytes(part(theirs[col], col, index(col, off), half), par_send.at[s])
    own.wait()
    wait_bytes(dxr.at[pl.ds(0, HEADS - 1)], a2a_send)
    wait_bytes(dxr.at[pl.ds(0, HEADS - 1)], a2a_recv)


def scatter(pz, px, py, dxr):
    any_ = pl.BlockSpec(memory_space=pl.ANY)
    vmem = pl.BlockSpec(memory_space=pltpu.VMEM)
    shape = jax.ShapeDtypeStruct
    dma = pltpu.SemaphoreType.DMA
    blocks = [pltpu.VMEM((n, m, 32, w), BF16) for _, n, m, w in COLOURS]
    rings = [pltpu.VMEM((2 * n, m // 2, 32, w), BF16) for _, n, m, w in COLOURS]
    planes = [pltpu.VMEM((m, 32, w), BF16) for _, n, m, w in COLOURS]
    return pl.pallas_call(
        scatter_kernel,
        out_shape=(shape((32, SEQ, 128), BF16), shape((32, 512), F32), shape((32, 128), F32)),
        in_specs=[any_] * 4,
        out_specs=(any_, vmem, vmem),
        scratch_shapes=blocks + blocks + rings + planes + [
            pltpu.VMEM((HIST, SEQ, 128), BF16),
            dma((32,)), dma((32,)), dma((32,)), dma((32,)), dma((32,)), dma((3,)), dma((3,)), dma, dma, dma((2,)),
        ],
        compiler_params=pltpu.CompilerParams(has_side_effects=True, vmem_limit_bytes=48 * 1024 * 1024),
        name="scatter",
    )(pz, px, py, dxr)


def local(events, cotangent, w_in, w_out, slot_source, slot_length):
    tab = jnp.full((8, 128), -1, jnp.int32).at[0, :32].set(slot_source).at[1, :32].set(slot_length)
    gz, gx, gy, xr, dr, tabs = gather(events, cotangent, w_in, w_out, tab)
    pz, px, py, dxr = layer(xr, dr, tabs, gz, gx, gy)
    return scatter(pz, px, py, dxr)


def solution(mesh):
    in_specs = (
        P("user", None, "tensor"),
        P("user", None, "tensor"),
        P("user", "tensor"),
        P("user", "tensor"),
        P("user"),
        P("user"),
    )
    out_specs = (P("user", None, "tensor"), P("user", "tensor"), P("user", "tensor"))
    return jax.shard_map(local, mesh=mesh, in_specs=in_specs, out_specs=out_specs, check_vma=False)
```

```python
import jax
import jax.numpy as jnp
from jax import lax
from jax.experimental import pallas as pl
from jax.experimental.pallas import tpu as pltpu
from jax.sharding import PartitionSpec as P

MESH = pl.DeviceIdType.MESH
F32 = jnp.float32
BF16 = jnp.bfloat16
EPS = 1e-05
HD = 128
SEQ = 128
HEADS = 8
NX, NY, NZ = 4, 4, 8
HIST = 4
ROWS = HIST * SEQ
D = 1024

COLOURS = ((2, NZ, 8, 384), (0, NX, 16, 128), (1, NY, 16, 128))
ORDER = (1, 2, 0)
BASE = (0, 16, 24)


def device_of(x, y, z, c):
    return ((lax.rem(x, 2) * NZ + z) * 2 + c, y * 2 + x // 2)


def remote(src, dst, send, recv, device):
    return pltpu.make_async_remote_copy(
        src_ref=src, dst_ref=dst, send_sem=send, recv_sem=recv, device_id=device, device_id_type=MESH
    )


def wait_bytes(ref, sem):
    pltpu.make_async_copy(ref, ref, sem).wait()


def silu_parts(v):
    sig = jax.nn.sigmoid(v)
    return v * sig, sig * (1.0 + v * (1.0 - sig))


def dot(a, b, dims):
    return lax.dot_general(a, b, (dims, ((), ())), preferred_element_type=F32)


NN, NT, TN = ((1,), (0,)), ((1,), (1,)), ((0,), (0,))


def when(cond, f):
    if isinstance(cond, bool):
        if cond:
            f()
    else:
        pl.when(cond)(f)


def kernel(
    ev, ct, w_in, w_out, tab, grad_x, grad_wi, grad_wo,
    gz, gx, gy, pz, px, py, tz, tx, ty, rz, rx, ry, s1z, s1x, s1y, s2z, s2x, s2y,
    xr, dr, tabs, nf, nb, nbt, dm, dmt, rstd_s, dn, wh, wo, dz_s, hb_s,
    loc, st1_send, st1_recv, st2_send, z2_send, z2_recv, x2_recv, y2_recv, ag_send, ag_recv, fw_send, fw_recv,
    a2a_send, a2a_recv, tab_send, tab_recv, par_send, par_recv, rs_send, rs_recv,
    o1_send, o1z_send, o1_recv, o1z_recv, o2_send, o2_recv, out_send, out_recv,
):
    u = lax.axis_index("user")
    t = lax.axis_index("tensor")
    c = lax.rem(u, 2)
    z = lax.rem(u // 2, NZ)
    x_lo = u // (2 * NZ)
    x_hi = lax.rem(t, 2)
    y = t // 2
    x = x_hi * 2 + x_lo
    mine = lax.rem(y + x_hi, 2)
    partner = (u + 1 - 2 * c, t)
    gs, ps, ts, rings = (gz, gx, gy), (pz, px, py), (tz, tx, ty), (rz, rx, ry)
    place = (z, x, y)

    def x_peer(i):
        return lax.rem(x + i, NX)

    def y_peer(i):
        return lax.rem(y + i, NY)

    def z_peer(i):
        return lax.rem(z + i, NZ)

    def ring_device(col, step):
        pos = [x, y, z]
        axis, n = COLOURS[col][:2]
        pos[axis] = lax.rem(pos[axis] + step + n, n)
        return device_of(*pos, c)

    barrier = pltpu.get_barrier_semaphore()

    def greet(device):
        pl.semaphore_signal(barrier, inc=1, device_id=device, device_id_type=MESH)

    greet(partner)
    for i in range(1, NX):
        greet(device_of(x_peer(i), y, z, c))
    for i in range(1, NY):
        greet(device_of(x, y_peer(i), z, c))
        greet((u, y_peer(i) * 2 + 1 - x_hi))
    for i in range(1, NZ):
        greet(device_of(x, y, z_peer(i), c))
    pl.semaphore_wait(barrier, 17)

    pieces = (w_in.at[:, pl.ds(0, 384)], w_in.at[:, pl.ds(384, 128)], w_out)
    slots = (
        gz.at[c, mine, z, y * 2 + x_lo],
        gx.at[c, mine, x, (y // 2) * NZ + z],
        gy.at[c, mine, y, x_lo * NZ + z],
    )
    own = [pltpu.make_async_copy(pieces[k], slots[k], loc.at[k]) for k in range(3)]
    own.append(pltpu.make_async_copy(tab, tabs.at[c, x_lo, z], loc.at[3]))
    for copy in own:
        copy.start()
    for i in range(1, NZ):
        device = device_of(x, y, z_peer(i), c)
        for col in (1, 2):
            remote(pieces[col], slots[col], st1_send.at[col], st1_recv.at[col], device).start()
    for i in range(1, NX):
        remote(pieces[0], slots[0], st1_send.at[0], st1_recv.at[0], device_of(x_peer(i), y, z, c)).start()
    for i in range(1, NZ):
        remote(tab, tabs.at[c, x_lo, z], tab_send.at[0], tab_recv.at[0], device_of(x, y, z_peer(i), c)).start()
    for copy in own:
        copy.wait()

    line_x = gx.at[c, mine, x, pl.ds((y // 2) * NZ, NZ)]
    line_y = gy.at[c, mine, y, pl.ds(x_lo * NZ, NZ)]
    wait_bytes(gx.at[c, mine, x, pl.ds(0, NZ - 1)], st1_recv.at[1])
    for i in range(1, NY):
        remote(line_x, line_x, st2_send.at[1], x2_recv.at[y], device_of(x, y_peer(i), z, c)).start()
    wait_bytes(gy.at[c, mine, y, pl.ds(0, NZ - 1)], st1_recv.at[2])
    for i in range(1, NX):
        remote(line_y, line_y, st2_send.at[2], y2_recv.at[x], device_of(x_peer(i), y, z, c)).start()
    wait_bytes(gz.at[c, 0, z, pl.ds(0, NX - 1)], st1_recv.at[0])
    for g in range(2):
        line_z = gz.at[c, g, z, pl.ds(y * 2, 2)]
        for i in range(1, NY):
            remote(line_z, line_z, z2_send.at[g], z2_recv.at[g], device_of(x, y_peer(i), z, c)).start()

    for k, (src, dst) in enumerate(((ev, xr), (ct, dr))):
        pltpu.make_async_copy(src.at[pl.ds(t * HIST, HIST)], dst.at[t], loc.at[4 + k]).start()
        for i in range(1, HEADS):
            q = lax.rem(t + i, HEADS)
            remote(src.at[pl.ds(q * HIST, HIST)], dst.at[t], a2a_send.at[k], a2a_recv.at[k], (u, q)).start()

    wait_bytes(tabs.at[c, x_lo, pl.ds(0, NZ - 1)], tab_recv.at[0])
    rows_tab = tabs.at[c, x_lo]
    remote(rows_tab, rows_tab, tab_send.at[1], tab_recv.at[1], device_of(x + 1 - 2 * x_lo, y, z, c)).start()

    def half_of(ref, half, m):
        return ref.at[pl.ds(half * (m // 2), m // 2)]

    def ring_sem(g, col, k, direction, half):
        return g * 32 + BASE[col] + (direction * (COLOURS[col][1] // 2) + k) * 2 + half

    def block(col, g, idx, half):
        return half_of(gs[col].at[c, g, idx], half, COLOURS[col][2])

    def forward(col, g, idx, half):
        part = block(col, g, idx, half)
        remote(part, part, fw_send.at[g * 3 + col], fw_recv.at[g * 3 + col], partner).start()

    def ag_send_part(col, g, k, direction, half):
        n = COLOURS[col][1]
        step = 1 - 2 * direction
        part = block(col, g, lax.rem(place[col] - step * k + n, n), half)
        s = ring_sem(g, col, k, direction, half)
        remote(part, part, ag_send.at[s], ag_recv.at[s], ring_device(col, step)).start()

    def ag_start(g):
        for col in ORDER:
            m = COLOURS[col][2]
            if col == 0:
                wait_bytes(gz.at[c, g, z, pl.ds(0, 6)], z2_recv.at[g])
            elif col == 1:
                for yy in range(2):
                    src = yy * 2 + lax.rem(g + x_hi, 2)
                    pl.when(src != y)(lambda: wait_bytes(gx.at[c, g, x, pl.ds(yy * NZ, NZ)], x2_recv.at[src]))
            else:
                for xl in range(2):
                    src = lax.rem(g + y, 2) * 2 + xl
                    pl.when(src != x)(lambda: wait_bytes(gy.at[c, g, y, pl.ds(xl * NZ, NZ)], y2_recv.at[src]))
            for half in (0, 1):
                for direction in (0, 1):
                    ag_send_part(col, g, 0, direction, half)
            for half in (0, 1):
                forward(col, g, place[col], half)

    def ag_step(g, k):
        for col in ORDER:
            n = COLOURS[col][1]
            last = n // 2 - 1

            def part_step(half, direction):
                step = 1 - 2 * direction
                idx = lax.rem(place[col] - step * (k + 1) + n, n)
                wait_bytes(block(col, g, idx, half), ag_recv.at[ring_sem(g, col, k, direction, half)])
                forward(col, g, idx, half)
                more = k + 1 <= last if half == direction else k + 1 < last
                when(more, lambda: ag_send_part(col, g, k + 1, direction, half))

            for half in (0, 1):
                for direction in (0, 1):
                    active = k <= last if half == direction else k < last
                    when(active, lambda: part_step(half, direction))

    def ag_done(g):
        for col in range(3):
            wait_bytes(gs[col].at[1 - c, g], fw_recv.at[g * 3 + col])

    def norm_rows():
        pltpu.make_async_copy(xr.at[t], xr.at[t], loc.at[4]).wait()
        wait_bytes(xr.at[pl.ds(0, HEADS - 1)], a2a_recv.at[0])
        for i in range(HIST):
            rows = pl.ds(i * SEQ, SEQ)
            xs = jnp.concatenate([xr[k, i] for k in range(HEADS)], axis=1).astype(F32)
            cen = xs - jnp.mean(xs, axis=1, keepdims=True)
            rstd = lax.rsqrt(jnp.mean(cen * cen, axis=1, keepdims=True) + EPS)
            nfi = cen * rstd
            nf[rows, :] = nfi
            rstd_s[rows, :] = jnp.broadcast_to(rstd, (SEQ, 128))
            nbi = nfi.astype(BF16)
            nb[rows, :] = nbi
            nbt[:, rows] = nbi.T

    def mask_rows():
        pltpu.make_async_copy(dr.at[t], dr.at[t], loc.at[5]).wait()
        wait_bytes(dr.at[pl.ds(0, HEADS - 1)], a2a_recv.at[1])
        wait_bytes(tabs.at[1 - c], tab_recv.at[2])
        lens = jnp.zeros((1, 128), F32)
        for cc in range(2):
            for xl in range(2):
                rows = tabs[cc, xl]
                lens = lens + jnp.sum(
                    jnp.where(rows[:, 0, :] == u, rows[:, 1, :], 0).astype(F32), axis=0, keepdims=True
                )
        lane = lax.broadcasted_iota(jnp.int32, (1, 128), 1)
        pos = lax.broadcasted_iota(jnp.int32, (SEQ, D), 0).astype(F32)
        for i in range(HIST):
            rows = pl.ds(i * SEQ, SEQ)
            length = jnp.sum(jnp.where(lane == t * HIST + i, lens, 0.0), axis=1, keepdims=True)
            di = jnp.concatenate([dr[k, i] for k in range(HEADS)], axis=1).astype(F32)
            di = jnp.where(pos < length, di, 0.0).astype(BF16)
            dm[rows, :] = di
            dmt[:, rows] = di.T
        dn[...] = jnp.zeros_like(dn)

    def head(g, hy):
        hx = lax.rem(g + hy, 2)
        for xl in range(2):
            for zz in range(NZ):
                for cc in range(2):
                    r = pl.ds(((xl * NZ + zz) * 2 + cc) * 32, 32)
                    wh[r, pl.ds(0, 384)] = gz[cc, g, zz, hy * 2 + xl]
                    wh[r, pl.ds(384, 128)] = gx[cc, g, hx * 2 + xl, (hy // 2) * NZ + zz]
                    wo[r, :] = gy[cc, g, hy, xl * NZ + zz]
        scale = HD ** (-0.5)
        zv = dot(nb[...], wh[...], NN)
        gv, sg = silu_parts(zv)
        gv = gv.astype(BF16)
        grad_h = dot(dm[...], wo[...], NN)
        uf = gv[:, 0:128].astype(F32)
        vp, qp, kp = gv[:, 128:256], gv[:, 256:384], gv[:, 384:512]
        hs = [slice(i * SEQ, i * SEQ + SEQ) for i in range(HIST)]

        def each(f):
            return jnp.concatenate([f(r) for r in hs], axis=0)

        s = each(lambda r: dot(qp[r], kp[r], NT)) * scale
        causal = lax.broadcasted_iota(jnp.int32, (SEQ, SEQ), 1) <= lax.broadcasted_iota(jnp.int32, (SEQ, SEQ), 0)
        causal = jnp.concatenate([causal] * HIST, axis=0)
        ss, sgs = silu_parts(s)
        at = jnp.where(causal, ss / SEQ, 0.0).astype(BF16)
        yv = each(lambda r: dot(at[r], vp[r], NN))
        ycen = yv - jnp.mean(yv, axis=1, keepdims=True)
        yrstd = lax.rsqrt(jnp.mean(ycen * ycen, axis=1, keepdims=True) + EPS)
        yn = ycen * yrstd
        hb_s[...] = (yn * uf).astype(BF16)
        dz_s[:, 0:128] = (grad_h * yn * sg[:, 0:128]).astype(BF16)
        gyn = grad_h * uf
        dy = (
            (gyn - jnp.mean(gyn, axis=1, keepdims=True) - yn * jnp.mean(gyn * yn, axis=1, keepdims=True)) * yrstd
        ).astype(BF16)
        da = each(lambda r: dot(dy[r], vp[r], NT))
        dz_s[:, 128:256] = (each(lambda r: dot(at[r], dy[r], TN)) * sg[:, 128:256]).astype(BF16)
        ds_ = jnp.where(causal, da * sgs * (scale / SEQ), 0.0).astype(BF16)
        dz_s[:, 256:384] = (each(lambda r: dot(ds_[r], kp[r], NN)) * sg[:, 256:384]).astype(BF16)
        dz_s[:, 384:512] = (each(lambda r: dot(ds_[r], qp[r], TN)) * sg[:, 384:512]).astype(BF16)
        for j in range(4):
            gw = dot(nbt[pl.ds(j * 256, 256), :], dz_s[...], NN).astype(BF16)
            go = dot(dmt[pl.ds(j * 256, 256), :], hb_s[...], NN).astype(BF16)
            for k in range(8):
                uu = j * 8 + k
                cc, zz, xl = uu % 2, (uu // 2) % NZ, uu // (2 * NZ)
                pz[cc, g, zz, hy * 2 + xl] = gw[k * 32 : k * 32 + 32, 0:384]
                px[cc, g, hx * 2 + xl, (hy // 2) * NZ + zz] = gw[k * 32 : k * 32 + 32, 384:512]
                py[cc, g, hy, xl * NZ + zz] = go[k * 32 : k * 32 + 32, :]
            dn[:, pl.ds(j * 256, 256)] += dot(dz_s[...], wh[pl.ds(j * 256, 256), :], NT)

    def rows_out():
        for i in range(HIST):
            rows = pl.ds(i * SEQ, SEQ)
            dni, nfi = dn[rows, :], nf[rows, :]
            branch = (
                dni - jnp.mean(dni, axis=1, keepdims=True) - nfi * jnp.mean(dni * nfi, axis=1, keepdims=True)
            ) * rstd_s[rows, 0:1]
            out = (dm[rows, :].astype(F32) + branch).astype(BF16)
            for k in range(HEADS):
                dr[k, i] = out[:, k * 128 : k * 128 + 128]

    def index(col, off):
        n = COLOURS[col][1]
        return lax.rem(place[col] + off + n, n)

    def par_sem(g, col, off, half):
        n = COLOURS[col][1]
        return g * 32 + BASE[col] + lax.rem(off + n, n) * 2 + half

    def rs_start(g):
        for j in range(NZ // 2 + 1):
            for col in ORDER:
                n, m = COLOURS[col][1:3]
                if j > n // 2:
                    continue
                for off in sorted({(n // 2 - j) % n, (j - n // 2) % n}):
                    for half in (0, 1):
                        s = par_sem(g, col, off, half)
                        remote(
                            half_of(ps[col].at[1 - c, g, index(col, off)], half, m),
                            half_of(ts[col].at[g, index(col, off)], half, m),
                            par_send.at[s], par_recv.at[s], partner,
                        ).start()

    def rs_add(g, col, off, half, from_ring):
        m = COLOURS[col][2]
        own_part = half_of(ps[col].at[c, g, index(col, off)], half, m)
        other = half_of(ts[col].at[g, index(col, off)], half, m)
        wait_bytes(other, par_recv.at[par_sem(g, col, off, half)])
        got = []
        for k, direction in from_ring:
            s = ring_sem(g, col, k, direction, half)
            wait_bytes(rings[col].at[s - BASE[col] - g * 32 + g * 2 * COLOURS[col][1]], rs_recv.at[s])
            got.append(rings[col].at[s - BASE[col] - g * 32 + g * 2 * COLOURS[col][1]])

        @pl.loop(0, m // 2)
        def _(i):
            v = own_part[i].astype(F32) + other[i].astype(F32)
            for ref in got:
                v = v + ref[i].astype(F32)
            own_part[i] = v.astype(BF16)

    def rs_step(g, k):
        for col in ORDER:
            n, m = COLOURS[col][1:3]
            top = n // 2

            def part_step(half, direction, from_ring):
                off = top - k if direction == 0 else k - top
                rs_add(g, col, off, half, ((k - 1, direction),) if from_ring else ())
                s = ring_sem(g, col, k, direction, half)
                remote(
                    half_of(ps[col].at[c, g, index(col, off)], half, m),
                    rings[col].at[s - BASE[col] - g * 32 + g * 2 * n],
                    rs_send.at[s], rs_recv.at[s], ring_device(col, 1 - 2 * direction),
                ).start()

            for half in (0, 1):
                for direction in (0, 1):
                    first = 0 if half == direction else 1
                    when(k == first, lambda: part_step(half, direction, False))
                    if isinstance(k, int):
                        when(first < k < top, lambda: part_step(half, direction, True))
                    elif first + 1 < top:
                        pl.when((k > first) & (k < top))(lambda: part_step(half, direction, True))

    def rs_lines(g):
        for col in ORDER:
            n = COLOURS[col][1]
            for half in (0, 1):
                rs_add(g, col, 0, half, tuple((n // 2 - 1, d) for d in (0, 1)))
        for i in range(1, NY):
            q = y_peer(i)
            device = device_of(x, q, z, c)

            @pl.when(lax.rem(q + x_hi, 2) == g)
            def _():
                remote(
                    px.at[c, g, x, pl.ds((q // 2) * NZ, NZ)], s1x.at[y], o1_send.at[0], o1_recv.at[0], device
                ).start()

        for i in range(1, NX):
            q = x_peer(i)
            device = device_of(q, y, z, c)

            @pl.when(lax.rem(y + q // 2, 2) == g)
            def _():
                remote(
                    py.at[c, g, y, pl.ds(lax.rem(q, 2) * NZ, NZ)], s1y.at[x], o1_send.at[1], o1_recv.at[1], device
                ).start()

        for i in range(1, NY):
            q = y_peer(i)
            remote(
                pz.at[c, g, z, pl.ds(q * 2, 2)], s1z.at[g, y], o1z_send.at[g], o1z_recv.at[g],
                device_of(x, q, z, c),
            ).start()

    def sum_into(own_part, parts, count):
        @pl.loop(0, count)
        def _(i):
            v = own_part[i].astype(F32)
            for ref in parts:
                v = v + ref[i].astype(F32)
            own_part[i] = v.astype(BF16)

    ag_start(0)
    ag_step(0, 0)
    wait_bytes(tabs.at[c, 1 - x_lo], tab_recv.at[1])
    remote(tabs.at[c], tabs.at[c], tab_send.at[2], tab_recv.at[2], partner).start()
    ag_step(0, 1)
    ag_step(0, 2)
    ag_start(1)
    norm_rows()
    ag_step(0, 3)
    mask_rows()
    ag_done(0)

    @pl.loop(0, NY)
    def _(j):
        head(0, j)
        ag_step(1, j)

    rs_start(0)
    ag_done(1)

    @pl.loop(0, NY)
    def _(j):
        head(1, j)
        rs_step(0, j)

    rs_start(1)
    rows_out()
    for i in range(1, HEADS):
        q = lax.rem(t + i, HEADS)
        remote(dr.at[q], grad_x.at[pl.ds(t * HIST, HIST)], out_send, out_recv, (u, q)).start()
    pltpu.make_async_copy(dr.at[t], grad_x.at[pl.ds(t * HIST, HIST)], loc.at[6]).start()
    rs_lines(0)
    for k in range(NZ // 2):
        rs_step(1, k)
    rs_lines(1)

    wait_bytes(s1x.at[pl.ds(0, NY - 1)], o1_recv.at[0])
    line_px = px.at[c, mine, x, pl.ds((y // 2) * NZ, NZ)]
    sum_into(line_px, [s1x.at[y_peer(i)] for i in range(1, NY)], NZ)
    for i in range(1, NZ):
        q = z_peer(i)
        remote(line_px.at[q], s2x.at[z], o2_send.at[1], o2_recv.at[1], device_of(x, y, q, c)).start()
    wait_bytes(s1y.at[pl.ds(0, NX - 1)], o1_recv.at[1])
    line_py = py.at[c, mine, y, pl.ds(x_lo * NZ, NZ)]
    sum_into(line_py, [s1y.at[x_peer(i)] for i in range(1, NX)], NZ)
    for i in range(1, NZ):
        q = z_peer(i)
        remote(line_py.at[q], s2y.at[z], o2_send.at[2], o2_recv.at[2], device_of(x, y, q, c)).start()
    for g in range(2):
        wait_bytes(s1z.at[g, pl.ds(0, NY - 1)], o1z_recv.at[g])
        sum_into(pz.at[c, g, z, pl.ds(y * 2, 2)], [s1z.at[g, y_peer(i)] for i in range(1, NY)], 2)
    for i in range(1, NX):
        q = x_peer(i)
        remote(
            pz.at[c, lax.rem(y + q // 2, 2), z, y * 2 + lax.rem(q, 2)], s2z.at[x], o2_send.at[0], o2_recv.at[0],
            device_of(q, y, z, c),
        ).start()

    wait_bytes(s2x.at[pl.ds(0, NZ - 1)], o2_recv.at[1])
    total = line_px[z].astype(F32)
    for i in range(1, NZ):
        total = total + s2x[z_peer(i)].astype(F32)
    grad_wi[:, pl.ds(384, 128)] = total
    wait_bytes(s2y.at[pl.ds(0, NZ - 1)], o2_recv.at[2])
    total = line_py[z].astype(F32)
    for i in range(1, NZ):
        total = total + s2y[z_peer(i)].astype(F32)
    grad_wo[...] = total
    wait_bytes(s2z.at[pl.ds(0, NX - 1)], o2_recv.at[0])
    total = pz[c, mine, z, y * 2 + x_lo].astype(F32)
    for i in range(1, NX):
        total = total + s2z[x_peer(i)].astype(F32)
    grad_wi[:, pl.ds(0, 384)] = total

    wait_bytes(gx.at[c, mine, x, pl.ds(0, NZ - 1)], st1_send.at[1])
    wait_bytes(gy.at[c, mine, y, pl.ds(0, NZ - 1)], st1_send.at[2])
    wait_bytes(gz.at[c, 0, z, pl.ds(0, NX - 1)], st1_send.at[0])
    wait_bytes(s1x.at[pl.ds(0, NY - 1)], st2_send.at[1])
    wait_bytes(s1y.at[pl.ds(0, NX - 1)], st2_send.at[2])
    for g in range(2):
        wait_bytes(gz.at[c, g, z, pl.ds(0, 6)], z2_send.at[g])
        wait_bytes(s1z.at[g, pl.ds(0, NY - 1)], o1z_send.at[g])
    wait_bytes(tabs.at[c, x_lo, pl.ds(0, NZ - 1)], tab_send.at[0])
    wait_bytes(tabs.at[c, x_lo], tab_send.at[1])
    wait_bytes(tabs.at[c], tab_send.at[2])
    wait_bytes(s1x.at[pl.ds(0, NY - 1)], o1_send.at[0])
    wait_bytes(s1y.at[pl.ds(0, NX - 1)], o1_send.at[1])
    wait_bytes(s2z.at[pl.ds(0, NX - 1)], o2_send.at[0])
    wait_bytes(s2x.at[pl.ds(0, NZ - 1)], o2_send.at[1])
    wait_bytes(s2y.at[pl.ds(0, NZ - 1)], o2_send.at[2])
    for k, ref in enumerate((xr, dr)):
        wait_bytes(ref.at[pl.ds(0, HEADS - 1)], a2a_send.at[k])
    for g in range(2):
        for col in range(3):
            n, m = COLOURS[col][1:3]
            wait_bytes(gs[col].at[c, g], fw_send.at[g * 3 + col])
            for half in (0, 1):
                for direction in (0, 1):
                    for k in range(n // 2):
                        s = ring_sem(g, col, k, direction, half)
                        part = half_of(gs[col].at[c, g, 0], half, m)
                        if half == direction or k < n // 2 - 1:
                            wait_bytes(part, ag_send.at[s])
                        if half == direction or k > 0:
                            wait_bytes(part, rs_send.at[s])
                for off in range(n):
                    wait_bytes(half_of(ts[col].at[g, 0], half, m), par_send.at[par_sem(g, col, off, half)])
    pltpu.make_async_copy(dr.at[t], grad_x.at[pl.ds(t * HIST, HIST)], loc.at[6]).wait()
    wait_bytes(dr.at[pl.ds(0, HEADS - 1)], out_send)
    wait_bytes(dr.at[pl.ds(0, HEADS - 1)], out_recv)


def local(events, cotangent, w_in, w_out, slot_source, slot_length):
    tab = jnp.pad(jnp.stack([slot_source, slot_length]), ((0, 6), (0, 96)))
    any_ = pl.BlockSpec(memory_space=pl.ANY)
    vmem = pl.BlockSpec(memory_space=pltpu.VMEM)
    shape = jax.ShapeDtypeStruct
    dma = pltpu.SemaphoreType.DMA
    both = [pltpu.VMEM((2, 2, n, m, 32, w), BF16) for _, n, m, w in COLOURS]
    theirs = [pltpu.VMEM((2, n, m, 32, w), BF16) for _, n, m, w in COLOURS]
    rings = [pltpu.VMEM((4 * n, m // 2, 32, w), BF16) for _, n, m, w in COLOURS]
    lines = [
        pltpu.VMEM((2, NY, 2, 32, 384), BF16),
        pltpu.VMEM((NY, NZ, 32, 128), BF16),
        pltpu.VMEM((NX, NZ, 32, 128), BF16),
        pltpu.VMEM((NX, 32, 384), BF16),
        pltpu.VMEM((NZ, 32, 128), BF16),
        pltpu.VMEM((NZ, 32, 128), BF16),
    ]
    work = [
        pltpu.VMEM((HEADS, HIST, SEQ, 128), BF16),
        pltpu.VMEM((HEADS, HIST, SEQ, 128), BF16),
        pltpu.VMEM((2, 2, NZ, 8, 128), jnp.int32),
        pltpu.VMEM((ROWS, D), F32),
        pltpu.VMEM((ROWS, D), BF16),
        pltpu.VMEM((D, ROWS), BF16),
        pltpu.VMEM((ROWS, D), BF16),
        pltpu.VMEM((D, ROWS), BF16),
        pltpu.VMEM((ROWS, 128), F32),
        pltpu.VMEM((ROWS, D), F32),
        pltpu.VMEM((D, 512), BF16),
        pltpu.VMEM((D, 128), BF16),
        pltpu.VMEM((ROWS, 512), BF16),
        pltpu.VMEM((ROWS, 128), BF16),
    ]
    sems = [
        dma((7,)), dma((3,)), dma((3,)), dma((3,)), dma((2,)), dma((2,)), dma((NY,)), dma((NX,)),
        dma((64,)), dma((64,)), dma((6,)), dma((6,)), dma((2,)), dma((2,)), dma((3,)), dma((3,)),
        dma((64,)), dma((64,)), dma((64,)), dma((64,)),
        dma((2,)), dma((2,)), dma((2,)), dma((2,)), dma((3,)), dma((3,)), dma, dma,
    ]
    return pl.pallas_call(
        kernel,
        out_shape=(shape((32, SEQ, 128), BF16), shape((32, 512), F32), shape((32, 128), F32)),
        in_specs=[any_, any_, vmem, vmem, vmem],
        out_specs=(any_, vmem, vmem),
        scratch_shapes=both + both + theirs + rings + lines + work + sems,
        compiler_params=pltpu.CompilerParams(
            has_side_effects=True, collective_id=0, vmem_limit_bytes=64 * 1024 * 1024 - 131072
        ),
        name="step",
    )(events, cotangent, w_in, w_out, tab)


def solution(mesh):
    in_specs = (
        P("user", None, "tensor"),
        P("user", None, "tensor"),
        P("user", "tensor"),
        P("user", "tensor"),
        P("user"),
        P("user"),
    )
    out_specs = (P("user", None, "tensor"), P("user", "tensor"), P("user", "tensor"))
    return jax.shard_map(local, mesh=mesh, in_specs=in_specs, out_specs=out_specs, check_vma=False)
```

```python
import jax
import jax.numpy as jnp
from jax import lax
from jax.experimental import pallas as pl
from jax.experimental.pallas import tpu as pltpu
from jax.sharding import PartitionSpec as P

MESH = pl.DeviceIdType.MESH
F32 = jnp.float32
BF16 = jnp.bfloat16
EPS = 1e-05
HD = 128
SEQ = 128
HEADS = 8
NX, NY, NZ = 4, 4, 8
HIST = 4
ROWS = HIST * SEQ
D = 1024

COLOURS = ((2, NZ, 8, 384), (0, NX, 16, 128), (1, NY, 16, 128))
ZM = 8


def device_of(x, y, z, c):
    return ((lax.rem(x, 2) * NZ + z) * 2 + c, y * 2 + x // 2)


def remote(src, dst, send, recv, device):
    return pltpu.make_async_remote_copy(
        src_ref=src, dst_ref=dst, send_sem=send, recv_sem=recv, device_id=device, device_id_type=MESH
    )


def wait_bytes(ref, sem):
    pltpu.make_async_copy(ref, ref, sem).wait()


def silu_parts(v):
    sig = jax.nn.sigmoid(v)
    return v * sig, sig * (1.0 + v * (1.0 - sig))


def dot(a, b, dims):
    return lax.dot_general(a, b, (dims, ((), ())), preferred_element_type=F32)


NN, NT, TN = ((1,), (0,)), ((1,), (1,)), ((0,), (0,))


def when(cond, f):
    if isinstance(cond, bool):
        if cond:
            f()
    else:
        pl.when(cond)(f)


def kernel(
    ev, ct, w_in, w_out, tab, grad_x, grad_wi, grad_wo,
    gz, gx, gy, pz, px, py, tz, tx, ty, rz, rx, ry, s1z, s1x, s1y, s2z, s2x, s2y,
    xr, dr, tabs, nf, nb, nbt, dm, dmt, rstd_s, dn, wh, wo, dz_s, hb_s,
    loc, st1_send, st1_recv, st2_send, z2_send, z2_recv, x2_recv, y2_recv, ag_send, ag_recv, fw_send, fw_recv,
    a2a_send, a2a_recv, tab_send, tab_recv, par_send, par_recv, rs_send, rs_recv,
    last_send, last_recv, rl_send, rl_recv,
    o1_send, o1z_send, o1_recv, o1z_recv, o2_send, o2_recv, out_send, out_recv,
):
    u = lax.axis_index("user")
    t = lax.axis_index("tensor")
    c = lax.rem(u, 2)
    z = lax.rem(u // 2, NZ)
    x_lo = u // (2 * NZ)
    x_hi = lax.rem(t, 2)
    y = t // 2
    x = x_hi * 2 + x_lo
    mine = lax.rem(y + x_hi, 2)
    partner = (u + 1 - 2 * c, t)
    gs, ps, ts, rings = (gz, gx, gy), (pz, px, py), (tz, tx, ty), (rz, rx, ry)
    place = (z, x, y)

    def x_peer(i):
        return lax.rem(x + i, NX)

    def y_peer(i):
        return lax.rem(y + i, NY)

    def z_peer(i):
        return lax.rem(z + i, NZ)

    def z_device(step):
        return device_of(x, y, lax.rem(z + step + NZ, NZ), c)

    def last_peer(col, i):
        q = x_peer(i) if col == 1 else y_peer(i)
        return q, device_of(q, y, z, c) if col == 1 else device_of(x, q, z, c)

    barrier = pltpu.get_barrier_semaphore()

    def greet(device):
        pl.semaphore_signal(barrier, inc=1, device_id=device, device_id_type=MESH)

    greet(partner)
    for i in range(1, NX):
        greet(device_of(x_peer(i), y, z, c))
    for i in range(1, NY):
        greet(device_of(x, y_peer(i), z, c))
        greet((u, y_peer(i) * 2 + 1 - x_hi))
    for i in range(1, NZ):
        greet(device_of(x, y, z_peer(i), c))
    pl.semaphore_wait(barrier, 17)

    pieces = (w_in.at[:, pl.ds(0, 384)], w_in.at[:, pl.ds(384, 128)], w_out)
    slots = (
        gz.at[c, mine, z, y * 2 + x_lo],
        gx.at[c, mine, x, (y // 2) * NZ + z],
        gy.at[c, mine, y, x_lo * NZ + z],
    )
    own = [pltpu.make_async_copy(pieces[k], slots[k], loc.at[k]) for k in range(3)]
    own.append(pltpu.make_async_copy(tab, tabs.at[c, x_lo, z], loc.at[3]))
    for copy in own:
        copy.start()
    for i in range(1, NX):
        remote(pieces[0], slots[0], st1_send.at[0], st1_recv.at[0], device_of(x_peer(i), y, z, c)).start()
    for i in range(1, NZ):
        device = device_of(x, y, z_peer(i), c)
        for col in (1, 2):
            remote(pieces[col], slots[col], st1_send.at[col], st1_recv.at[col], device).start()
    for i in range(1, NZ):
        remote(tab, tabs.at[c, x_lo, z], tab_send.at[0], tab_recv.at[0], device_of(x, y, z_peer(i), c)).start()
    for copy in own:
        copy.wait()

    def line_z(g):
        line = gz.at[c, g, z, pl.ds(y * 2, 2)]
        for i in range(1, NY):
            remote(line, line, z2_send.at[g], z2_recv.at[g], device_of(x, y_peer(i), z, c)).start()

    wait_bytes(gz.at[c, 0, z, pl.ds(0, NX - 1)], st1_recv.at[0])
    line_z(0)
    line_x = gx.at[c, mine, x, pl.ds((y // 2) * NZ, NZ)]
    line_y = gy.at[c, mine, y, pl.ds(x_lo * NZ, NZ)]
    wait_bytes(gx.at[c, mine, x, pl.ds(0, NZ - 1)], st1_recv.at[1])
    for i in range(1, NY):
        remote(line_x, line_x, st2_send.at[1], x2_recv.at[y], device_of(x, y_peer(i), z, c)).start()
    wait_bytes(gy.at[c, mine, y, pl.ds(0, NZ - 1)], st1_recv.at[2])
    for i in range(1, NX):
        remote(line_y, line_y, st2_send.at[2], y2_recv.at[x], device_of(x_peer(i), y, z, c)).start()
    line_z(1)

    def send_rows():
        for k, (src, dst) in enumerate(((ev, xr), (ct, dr))):
            pltpu.make_async_copy(src.at[pl.ds(t * HIST, HIST)], dst.at[t], loc.at[4 + k]).start()
            for i in range(1, HEADS):
                q = lax.rem(t + i, HEADS)
                remote(src.at[pl.ds(q * HIST, HIST)], dst.at[t], a2a_send.at[k], a2a_recv.at[k], (u, q)).start()

    wait_bytes(tabs.at[c, x_lo, pl.ds(0, NZ - 1)], tab_recv.at[0])
    rows_tab = tabs.at[c, x_lo]
    remote(rows_tab, rows_tab, tab_send.at[1], tab_recv.at[1], device_of(x + 1 - 2 * x_lo, y, z, c)).start()

    def half_of(ref, half):
        return ref.at[pl.ds(half * (ZM // 2), ZM // 2)]

    def ring_sem(g, k, direction, half):
        return g * 16 + (direction * (NZ // 2) + k) * 2 + half

    def block(g, idx, half):
        return half_of(gz.at[c, g, idx], half)

    def forward(col, g, part):
        remote(part, part, fw_send.at[g * 3 + col], fw_recv.at[g * 3 + col], partner).start()

    def ring_part(g, k, direction, half):
        step = 1 - 2 * direction
        part = block(g, lax.rem(z - step * k + NZ, NZ), half)
        s = ring_sem(g, k, direction, half)
        remote(part, part, ag_send.at[s], ag_recv.at[s], z_device(step)).start()

    def last_sem(g, col, q):
        return (g * 2 + col - 1) * 4 + q

    def ag_start_z(g):
        wait_bytes(gz.at[c, g, z, pl.ds(0, 6)], z2_recv.at[g])
        for half in (0, 1):
            for direction in (0, 1):
                ring_part(g, 0, direction, half)
        forward(0, g, gz.at[c, g, z])

    def ag_start_xy(g):
        for yy in range(2):
            src = yy * 2 + lax.rem(g + x_hi, 2)
            pl.when(src != y)(lambda: wait_bytes(gx.at[c, g, x, pl.ds(yy * NZ, NZ)], x2_recv.at[src]))
        for xl in range(2):
            src = lax.rem(g + y, 2) * 2 + xl
            pl.when(src != x)(lambda: wait_bytes(gy.at[c, g, y, pl.ds(xl * NZ, NZ)], y2_recv.at[src]))
        for col in (1, 2):
            part = gs[col].at[c, g, place[col]]
            for i in (1, 3, 2):
                s = last_sem(g, col, place[col])
                remote(part, part, last_send.at[g * 2 + col - 1], last_recv.at[s], last_peer(col, i)[1]).start()
            forward(col, g, part)

    def ag_take_xy(g):
        for i in (1, 3, 2):
            for col in (1, 2):
                q = last_peer(col, i)[0]
                part = gs[col].at[c, g, q]
                wait_bytes(part, last_recv.at[last_sem(g, col, q)])
                forward(col, g, part)

    def ag_step(g, k):
        last = NZ // 2 - 1

        def part_step(half, direction):
            step = 1 - 2 * direction
            idx = lax.rem(z - step * (k + 1) + NZ, NZ)
            wait_bytes(block(g, idx, half), ag_recv.at[ring_sem(g, k, direction, half)])
            more = k + 1 <= last if half == direction else k + 1 < last
            when(more, lambda: ring_part(g, k + 1, direction, half))
            forward(0, g, block(g, idx, half))

        for half in (0, 1):
            for direction in (0, 1):
                active = k <= last if half == direction else k < last
                when(active, lambda: part_step(half, direction))

    def ag_done(g):
        for col in range(3):
            wait_bytes(gs[col].at[1 - c, g], fw_recv.at[g * 3 + col])

    def norm_rows():
        pltpu.make_async_copy(xr.at[t], xr.at[t], loc.at[4]).wait()
        wait_bytes(xr.at[pl.ds(0, HEADS - 1)], a2a_recv.at[0])
        for i in range(HIST):
            rows = pl.ds(i * SEQ, SEQ)
            xs = jnp.concatenate([xr[k, i] for k in range(HEADS)], axis=1).astype(F32)
            cen = xs - jnp.mean(xs, axis=1, keepdims=True)
            rstd = lax.rsqrt(jnp.mean(cen * cen, axis=1, keepdims=True) + EPS)
            nfi = cen * rstd
            nf[rows, :] = nfi
            rstd_s[rows, :] = jnp.broadcast_to(rstd, (SEQ, 128))
            nbi = nfi.astype(BF16)
            nb[rows, :] = nbi
            nbt[:, rows] = nbi.T

    def mask_rows():
        pltpu.make_async_copy(dr.at[t], dr.at[t], loc.at[5]).wait()
        wait_bytes(dr.at[pl.ds(0, HEADS - 1)], a2a_recv.at[1])
        wait_bytes(tabs.at[1 - c], tab_recv.at[2])
        lens = jnp.zeros((1, 128), F32)
        for cc in range(2):
            for xl in range(2):
                rows = tabs[cc, xl]
                lens = lens + jnp.sum(
                    jnp.where(rows[:, 0, :] == u, rows[:, 1, :], 0).astype(F32), axis=0, keepdims=True
                )
        lane = lax.broadcasted_iota(jnp.int32, (1, 128), 1)
        pos = lax.broadcasted_iota(jnp.int32, (SEQ, D), 0).astype(F32)
        for i in range(HIST):
            rows = pl.ds(i * SEQ, SEQ)
            length = jnp.sum(jnp.where(lane == t * HIST + i, lens, 0.0), axis=1, keepdims=True)
            di = jnp.concatenate([dr[k, i] for k in range(HEADS)], axis=1).astype(F32)
            di = jnp.where(pos < length, di, 0.0).astype(BF16)
            dm[rows, :] = di
            dmt[:, rows] = di.T
        dn[...] = jnp.zeros_like(dn)

    def head(g, hy):
        hx = lax.rem(g + hy, 2)
        for xl in range(2):
            for zz in range(NZ):
                for cc in range(2):
                    r = pl.ds(((xl * NZ + zz) * 2 + cc) * 32, 32)
                    wh[r, pl.ds(0, 384)] = gz[cc, g, zz, hy * 2 + xl]
                    wh[r, pl.ds(384, 128)] = gx[cc, g, hx * 2 + xl, (hy // 2) * NZ + zz]
                    wo[r, :] = gy[cc, g, hy, xl * NZ + zz]
        scale = HD ** (-0.5)
        zv = dot(nb[...], wh[...], NN)
        gv, sg = silu_parts(zv)
        gv = gv.astype(BF16)
        grad_h = dot(dm[...], wo[...], NN)
        uf = gv[:, 0:128].astype(F32)
        vp, qp, kp = gv[:, 128:256], gv[:, 256:384], gv[:, 384:512]
        hs = [slice(i * SEQ, i * SEQ + SEQ) for i in range(HIST)]

        def each(f):
            return jnp.concatenate([f(r) for r in hs], axis=0)

        s = each(lambda r: dot(qp[r], kp[r], NT)) * scale
        causal = lax.broadcasted_iota(jnp.int32, (SEQ, SEQ), 1) <= lax.broadcasted_iota(jnp.int32, (SEQ, SEQ), 0)
        causal = jnp.concatenate([causal] * HIST, axis=0)
        ss, sgs = silu_parts(s)
        at = jnp.where(causal, ss / SEQ, 0.0).astype(BF16)
        yv = each(lambda r: dot(at[r], vp[r], NN))
        ycen = yv - jnp.mean(yv, axis=1, keepdims=True)
        yrstd = lax.rsqrt(jnp.mean(ycen * ycen, axis=1, keepdims=True) + EPS)
        yn = ycen * yrstd
        hb_s[...] = (yn * uf).astype(BF16)
        dz_s[:, 0:128] = (grad_h * yn * sg[:, 0:128]).astype(BF16)
        gyn = grad_h * uf
        dy = (
            (gyn - jnp.mean(gyn, axis=1, keepdims=True) - yn * jnp.mean(gyn * yn, axis=1, keepdims=True)) * yrstd
        ).astype(BF16)
        da = each(lambda r: dot(dy[r], vp[r], NT))
        dz_s[:, 128:256] = (each(lambda r: dot(at[r], dy[r], TN)) * sg[:, 128:256]).astype(BF16)
        ds_ = jnp.where(causal, da * sgs * (scale / SEQ), 0.0).astype(BF16)
        dz_s[:, 256:384] = (each(lambda r: dot(ds_[r], kp[r], NN)) * sg[:, 256:384]).astype(BF16)
        dz_s[:, 384:512] = (each(lambda r: dot(ds_[r], qp[r], TN)) * sg[:, 384:512]).astype(BF16)
        for j in range(4):
            gw = dot(nbt[pl.ds(j * 256, 256), :], dz_s[...], NN).astype(BF16)
            go = dot(dmt[pl.ds(j * 256, 256), :], hb_s[...], NN).astype(BF16)
            for k in range(8):
                uu = j * 8 + k
                cc, zz, xl = uu % 2, (uu // 2) % NZ, uu // (2 * NZ)
                pz[cc, g, zz, hy * 2 + xl] = gw[k * 32 : k * 32 + 32, 0:384]
                px[cc, g, hx * 2 + xl, (hy // 2) * NZ + zz] = gw[k * 32 : k * 32 + 32, 384:512]
                py[cc, g, hy, xl * NZ + zz] = go[k * 32 : k * 32 + 32, :]
            dn[:, pl.ds(j * 256, 256)] += dot(dz_s[...], wh[pl.ds(j * 256, 256), :], NT)

    def rows_out():
        for i in range(HIST):
            rows = pl.ds(i * SEQ, SEQ)
            dni, nfi = dn[rows, :], nf[rows, :]
            branch = (
                dni - jnp.mean(dni, axis=1, keepdims=True) - nfi * jnp.mean(dni * nfi, axis=1, keepdims=True)
            ) * rstd_s[rows, 0:1]
            out = (dm[rows, :].astype(F32) + branch).astype(BF16)
            for k in range(HEADS):
                dr[k, i] = out[:, k * 128 : k * 128 + 128]

    def head_parts(ref_of, g, hy):
        hx = lax.rem(g + hy, 2)
        return (
            ref_of(0).at[:, pl.ds(hy * 2, 2)],
            ref_of(1).at[pl.ds(hx * 2, 2), pl.ds((hy // 2) * NZ, NZ)],
            ref_of(2).at[hy],
        )

    def to_partner(g, hy):
        src = head_parts(lambda col: ps[col].at[1 - c, g], g, hy)
        dst = head_parts(lambda col: ts[col].at[g], g, hy)
        for col in range(3):
            s = (g * 3 + col) * 4 + hy
            remote(src[col], dst[col], par_send.at[s], par_recv.at[s], partner).start()

    def from_partner(g):
        for hy in range(NY):
            dst = head_parts(lambda col: ts[col].at[g], g, hy)
            for col in range(3):
                wait_bytes(dst[col], par_recv.at[(g * 3 + col) * 4 + hy])

    def add_parts(own_part, parts, count):
        step = min(count, 4 if own_part.shape[-1] == 128 else 2)

        @pl.loop(0, count // step)
        def _(i):
            rows = pl.ds(i * step, step)
            v = own_part[rows].astype(F32)
            for ref in parts:
                v = v + ref[rows].astype(F32)
            own_part[rows] = v.astype(BF16)

    def rs_add(g, off, half, from_ring):
        idx = lax.rem(z + off + NZ, NZ)
        parts = [half_of(tz.at[g, idx], half)]
        for k, direction in from_ring:
            s = ring_sem(g, k, direction, half)
            wait_bytes(rz.at[s], rs_recv.at[s])
            parts.append(rz.at[s])
        add_parts(half_of(pz.at[c, g, idx], half), parts, ZM // 2)

    def rs_step(g, k):
        top = NZ // 2

        def part_step(half, direction, from_ring):
            off = top - k if direction == 0 else k - top
            rs_add(g, off, half, ((k - 1, direction),) if from_ring else ())
            s = ring_sem(g, k, direction, half)
            remote(
                half_of(pz.at[c, g, lax.rem(z + off + NZ, NZ)], half), rz.at[s],
                rs_send.at[s], rs_recv.at[s], z_device(1 - 2 * direction),
            ).start()

        for half in (0, 1):
            for direction in (0, 1):
                first = 0 if half == direction else 1
                when(k == first, lambda: part_step(half, direction, False))
                if isinstance(k, int):
                    when(first < k < top, lambda: part_step(half, direction, True))
                else:
                    pl.when((k > first) & (k < top))(lambda: part_step(half, direction, True))

    def rs_send_xy(g):
        for i in (2, 1, 3):
            for col in (1, 2):
                q, device = last_peer(col, i)
                part = ps[col].at[c, g, q]
                add_parts(part, [ts[col].at[g, q]], COLOURS[col][2])
                s = last_sem(g, col, place[col])
                remote(
                    part, rings[col].at[g, place[col]], rl_send.at[g * 2 + col - 1], rl_recv.at[s], device
                ).start()

    def rs_take_xy(g):
        for col in (1, 2):
            parts = [ts[col].at[g, place[col]]]
            for i in (1, 3, 2):
                q = last_peer(col, i)[0]
                wait_bytes(rings[col].at[g, q], rl_recv.at[last_sem(g, col, q)])
                parts.append(rings[col].at[g, q])
            add_parts(ps[col].at[c, g, place[col]], parts, COLOURS[col][2])
        for i in range(1, NY):
            q = y_peer(i)
            device = device_of(x, q, z, c)

            @pl.when(lax.rem(q + x_hi, 2) == g)
            def _():
                remote(
                    px.at[c, g, x, pl.ds((q // 2) * NZ, NZ)], s1x.at[y], o1_send.at[0], o1_recv.at[0], device
                ).start()

        for i in range(1, NX):
            q = x_peer(i)
            device = device_of(q, y, z, c)

            @pl.when(lax.rem(y + q // 2, 2) == g)
            def _():
                remote(
                    py.at[c, g, y, pl.ds(lax.rem(q, 2) * NZ, NZ)], s1y.at[x], o1_send.at[1], o1_recv.at[1], device
                ).start()

    def rs_take_z(g):
        for half in (0, 1):
            rs_add(g, 0, half, tuple((NZ // 2 - 1, d) for d in (0, 1)))
        for i in range(1, NY):
            q = y_peer(i)
            remote(
                pz.at[c, g, z, pl.ds(q * 2, 2)], s1z.at[g, y], o1z_send.at[g], o1z_recv.at[g],
                device_of(x, q, z, c),
            ).start()

    ag_start_z(0)
    ag_start_xy(0)
    send_rows()
    ag_step(0, 0)
    wait_bytes(tabs.at[c, 1 - x_lo], tab_recv.at[1])
    remote(tabs.at[c], tabs.at[c], tab_send.at[2], tab_recv.at[2], partner).start()
    ag_step(0, 1)
    ag_step(0, 2)
    ag_start_z(1)
    ag_start_xy(1)
    ag_step(0, 3)
    ag_take_xy(0)
    norm_rows()
    ag_step(1, 0)
    mask_rows()
    ag_done(0)

    @pl.loop(0, NY)
    def _(j):
        head(0, j)
        to_partner(0, j)
        pl.when(j < NY - 1)(lambda: ag_step(1, j + 1))
        pl.when(j == 0)(lambda: ag_take_xy(1))

    ag_done(1)

    @pl.loop(0, NY)
    def _(j):
        head(1, j)
        to_partner(1, j)

        @pl.when(j == 0)
        def _():
            from_partner(0)
            rs_send_xy(0)

        rs_step(0, j)

    rows_out()
    from_partner(1)
    rs_step(1, 0)
    rs_send_xy(1)
    for i in range(1, HEADS):
        q = lax.rem(t + i, HEADS)
        remote(dr.at[q], grad_x.at[pl.ds(t * HIST, HIST)], out_send, out_recv, (u, q)).start()
    pltpu.make_async_copy(dr.at[t], grad_x.at[pl.ds(t * HIST, HIST)], loc.at[6]).start()
    rs_take_xy(0)
    rs_take_z(0)
    rs_step(1, 1)
    rs_step(1, 2)
    rs_step(1, 3)
    rs_take_xy(1)
    rs_take_z(1)

    wait_bytes(s1x.at[pl.ds(0, NY - 1)], o1_recv.at[0])
    line_px = px.at[c, mine, x, pl.ds((y // 2) * NZ, NZ)]
    add_parts(line_px, [s1x.at[y_peer(i)] for i in range(1, NY)], NZ)
    for i in range(1, NZ):
        q = z_peer(i)
        remote(line_px.at[q], s2x.at[z], o2_send.at[1], o2_recv.at[1], device_of(x, y, q, c)).start()
    wait_bytes(s1y.at[pl.ds(0, NX - 1)], o1_recv.at[1])
    line_py = py.at[c, mine, y, pl.ds(x_lo * NZ, NZ)]
    add_parts(line_py, [s1y.at[x_peer(i)] for i in range(1, NX)], NZ)
    for i in range(1, NZ):
        q = z_peer(i)
        remote(line_py.at[q], s2y.at[z], o2_send.at[2], o2_recv.at[2], device_of(x, y, q, c)).start()
    for g in range(2):
        wait_bytes(s1z.at[g, pl.ds(0, NY - 1)], o1z_recv.at[g])
        add_parts(pz.at[c, g, z, pl.ds(y * 2, 2)], [s1z.at[g, y_peer(i)] for i in range(1, NY)], 2)
    for i in range(1, NX):
        q = x_peer(i)
        remote(
            pz.at[c, lax.rem(y + q // 2, 2), z, y * 2 + lax.rem(q, 2)], s2z.at[x], o2_send.at[0], o2_recv.at[0],
            device_of(q, y, z, c),
        ).start()

    wait_bytes(s2x.at[pl.ds(0, NZ - 1)], o2_recv.at[1])
    total = line_px[z].astype(F32)
    for i in range(1, NZ):
        total = total + s2x[z_peer(i)].astype(F32)
    grad_wi[:, pl.ds(384, 128)] = total
    wait_bytes(s2y.at[pl.ds(0, NZ - 1)], o2_recv.at[2])
    total = line_py[z].astype(F32)
    for i in range(1, NZ):
        total = total + s2y[z_peer(i)].astype(F32)
    grad_wo[...] = total
    wait_bytes(s2z.at[pl.ds(0, NX - 1)], o2_recv.at[0])
    total = pz[c, mine, z, y * 2 + x_lo].astype(F32)
    for i in range(1, NX):
        total = total + s2z[x_peer(i)].astype(F32)
    grad_wi[:, pl.ds(0, 384)] = total

    wait_bytes(gx.at[c, mine, x, pl.ds(0, NZ - 1)], st1_send.at[1])
    wait_bytes(gy.at[c, mine, y, pl.ds(0, NZ - 1)], st1_send.at[2])
    wait_bytes(gz.at[c, 0, z, pl.ds(0, NX - 1)], st1_send.at[0])
    wait_bytes(s1x.at[pl.ds(0, NY - 1)], st2_send.at[1])
    wait_bytes(s1y.at[pl.ds(0, NX - 1)], st2_send.at[2])
    for g in range(2):
        wait_bytes(gz.at[c, g, z, pl.ds(0, 6)], z2_send.at[g])
        wait_bytes(s1z.at[g, pl.ds(0, NY - 1)], o1z_send.at[g])
    wait_bytes(tabs.at[c, x_lo, pl.ds(0, NZ - 1)], tab_send.at[0])
    wait_bytes(tabs.at[c, x_lo], tab_send.at[1])
    wait_bytes(tabs.at[c], tab_send.at[2])
    wait_bytes(s1x.at[pl.ds(0, NY - 1)], o1_send.at[0])
    wait_bytes(s1y.at[pl.ds(0, NX - 1)], o1_send.at[1])
    wait_bytes(s2z.at[pl.ds(0, NX - 1)], o2_send.at[0])
    wait_bytes(s2x.at[pl.ds(0, NZ - 1)], o2_send.at[1])
    wait_bytes(s2y.at[pl.ds(0, NZ - 1)], o2_send.at[2])
    for k, ref in enumerate((xr, dr)):
        wait_bytes(ref.at[pl.ds(0, HEADS - 1)], a2a_send.at[k])
    for g in range(2):
        for col in range(3):
            wait_bytes(gs[col].at[c, g], fw_send.at[g * 3 + col])
            for hy in range(NY):
                dst = head_parts(lambda k: ts[k].at[g], g, hy)
                wait_bytes(dst[col], par_send.at[(g * 3 + col) * 4 + hy])
        for col in (1, 2):
            wait_bytes(rings[col].at[g, pl.ds(0, 3)], last_send.at[g * 2 + col - 1])
            wait_bytes(rings[col].at[g, pl.ds(0, 3)], rl_send.at[g * 2 + col - 1])
        for half in (0, 1):
            for direction in (0, 1):
                for k in range(NZ // 2):
                    s = ring_sem(g, k, direction, half)
                    if half == direction or k < NZ // 2 - 1:
                        wait_bytes(rz.at[s], ag_send.at[s])
                    if half == direction or k > 0:
                        wait_bytes(rz.at[s], rs_send.at[s])
    pltpu.make_async_copy(dr.at[t], grad_x.at[pl.ds(t * HIST, HIST)], loc.at[6]).wait()
    wait_bytes(dr.at[pl.ds(0, HEADS - 1)], out_send)
    wait_bytes(dr.at[pl.ds(0, HEADS - 1)], out_recv)


def local(events, cotangent, w_in, w_out, slot_source, slot_length):
    tab = jnp.pad(jnp.stack([slot_source, slot_length]), ((0, 6), (0, 96)))
    any_ = pl.BlockSpec(memory_space=pl.ANY)
    vmem = pl.BlockSpec(memory_space=pltpu.VMEM)
    shape = jax.ShapeDtypeStruct
    dma = pltpu.SemaphoreType.DMA
    both = [pltpu.VMEM((2, 2, n, m, 32, w), BF16) for _, n, m, w in COLOURS]
    theirs = [pltpu.VMEM((2, n, m, 32, w), BF16) for _, n, m, w in COLOURS]
    rings = [pltpu.VMEM((32, ZM // 2, 32, 384), BF16)] + [pltpu.VMEM((2, n, m, 32, w), BF16) for _, n, m, w in COLOURS[1:]]
    lines = [
        pltpu.VMEM((2, NY, 2, 32, 384), BF16),
        pltpu.VMEM((NY, NZ, 32, 128), BF16),
        pltpu.VMEM((NX, NZ, 32, 128), BF16),
        pltpu.VMEM((NX, 32, 384), BF16),
        pltpu.VMEM((NZ, 32, 128), BF16),
        pltpu.VMEM((NZ, 32, 128), BF16),
    ]
    work = [
        pltpu.VMEM((HEADS, HIST, SEQ, 128), BF16),
        pltpu.VMEM((HEADS, HIST, SEQ, 128), BF16),
        pltpu.VMEM((2, 2, NZ, 8, 128), jnp.int32),
        pltpu.VMEM((ROWS, D), F32),
        pltpu.VMEM((ROWS, D), BF16),
        pltpu.VMEM((D, ROWS), BF16),
        pltpu.VMEM((ROWS, D), BF16),
        pltpu.VMEM((D, ROWS), BF16),
        pltpu.VMEM((ROWS, 128), F32),
        pltpu.VMEM((ROWS, D), F32),
        pltpu.VMEM((D, 512), BF16),
        pltpu.VMEM((D, 128), BF16),
        pltpu.VMEM((ROWS, 512), BF16),
        pltpu.VMEM((ROWS, 128), BF16),
    ]
    sems = [
        dma((7,)), dma((3,)), dma((3,)), dma((3,)), dma((2,)), dma((2,)), dma((NY,)), dma((NX,)),
        dma((32,)), dma((32,)), dma((6,)), dma((6,)), dma((2,)), dma((2,)), dma((3,)), dma((3,)),
        dma((24,)), dma((24,)), dma((32,)), dma((32,)), dma((4,)), dma((16,)), dma((4,)), dma((16,)),
        dma((2,)), dma((2,)), dma((2,)), dma((2,)), dma((3,)), dma((3,)), dma, dma,
    ]
    return pl.pallas_call(
        kernel,
        out_shape=(shape((32, SEQ, 128), BF16), shape((32, 512), F32), shape((32, 128), F32)),
        in_specs=[any_, any_, vmem, vmem, vmem],
        out_specs=(any_, vmem, vmem),
        scratch_shapes=both + both + theirs + rings + lines + work + sems,
        compiler_params=pltpu.CompilerParams(
            has_side_effects=True, collective_id=0, vmem_limit_bytes=64 * 1024 * 1024 - 131072
        ),
        name="step",
    )(events, cotangent, w_in, w_out, tab)


def solution(mesh):
    in_specs = (
        P("user", None, "tensor"),
        P("user", None, "tensor"),
        P("user", "tensor"),
        P("user", "tensor"),
        P("user"),
        P("user"),
    )
    out_specs = (P("user", None, "tensor"), P("user", "tensor"), P("user", "tensor"))
    return jax.shard_map(local, mesh=mesh, in_specs=in_specs, out_specs=out_specs, check_vma=False)
```

```python
import jax
import jax.numpy as jnp
from jax import lax
from jax.experimental import pallas as pl
from jax.experimental.pallas import tpu as pltpu
from jax.sharding import PartitionSpec as P

MESH = pl.DeviceIdType.MESH
F32 = jnp.float32
BF16 = jnp.bfloat16
EPS = 1e-05
HD = 128
SEQ = 128
HEADS = 8
NX, NY, NZ = 4, 4, 8
HIST = 4
ROWS = HIST * SEQ
D = 1024

COLOURS = ((2, NZ, 8, 384), (0, NX, 16, 128), (1, NY, 16, 128))
ZM = 8


def device_of(x, y, z, c):
    return ((lax.rem(x, 2) * NZ + z) * 2 + c, y * 2 + x // 2)


def remote(src, dst, send, recv, device):
    return pltpu.make_async_remote_copy(
        src_ref=src, dst_ref=dst, send_sem=send, recv_sem=recv, device_id=device, device_id_type=MESH
    )


def wait_bytes(ref, sem):
    pltpu.make_async_copy(ref, ref, sem).wait()


def silu_parts(v):
    sig = jax.nn.sigmoid(v)
    return v * sig, sig * (1.0 + v * (1.0 - sig))


def dot(a, b, dims):
    return lax.dot_general(a, b, (dims, ((), ())), preferred_element_type=F32)


NN, NT, TN = ((1,), (0,)), ((1,), (1,)), ((0,), (0,))


def when(cond, f):
    if isinstance(cond, bool):
        if cond:
            f()
    else:
        pl.when(cond)(f)


def kernel(
    ev, ct, w_in, w_out, tab, grad_x, grad_wi, grad_wo,
    gz, gx, gy, pz, px, py, tz, tx, ty, rz, rx, ry, s1z, s1x, s1y, s2z, s2x, s2y,
    xr, dr, tabs, nf, nb, nbt, dm, dmt, rstd_s, dn, wh, wo, dz_s, hb_s, z_s,
    loc, st1_send, st1_recv, st2_send, z2_send, z2_recv, x2_recv, y2_recv, ag_send, ag_recv, fw_send, fw_recv,
    a2a_send, a2a_recv, tab_send, tab_recv, par_send, par_recv, rs_send, rs_recv,
    last_send, last_recv, rl_send, rl_recv,
    o1_send, o1z_send, o1_recv, o1z_recv, o2_send, o2_recv, out_send, out_recv,
):
    u = lax.axis_index("user")
    t = lax.axis_index("tensor")
    c = lax.rem(u, 2)
    z = lax.rem(u // 2, NZ)
    x_lo = u // (2 * NZ)
    x_hi = lax.rem(t, 2)
    y = t // 2
    x = x_hi * 2 + x_lo
    mine = lax.rem(y + x_hi, 2)
    partner = (u + 1 - 2 * c, t)
    gs, ps, ts, rings = (gz, gx, gy), (pz, px, py), (tz, tx, ty), (rz, rx, ry)
    place = (z, x, y)

    def x_peer(i):
        return lax.rem(x + i, NX)

    def y_peer(i):
        return lax.rem(y + i, NY)

    def z_peer(i):
        return lax.rem(z + i, NZ)

    def z_device(step):
        return device_of(x, y, lax.rem(z + step + NZ, NZ), c)

    def last_peer(col, i):
        q = x_peer(i) if col == 1 else y_peer(i)
        return q, device_of(q, y, z, c) if col == 1 else device_of(x, q, z, c)

    barrier = pltpu.get_barrier_semaphore()

    def greet(device):
        pl.semaphore_signal(barrier, inc=1, device_id=device, device_id_type=MESH)

    greet(partner)
    for i in range(1, NX):
        greet(device_of(x_peer(i), y, z, c))
    for i in range(1, NY):
        greet(device_of(x, y_peer(i), z, c))
        greet((u, y_peer(i) * 2 + 1 - x_hi))
    for i in range(1, NZ):
        greet(device_of(x, y, z_peer(i), c))
    pl.semaphore_wait(barrier, 17)

    def send_rows(k):
        src, dst = ((ev, xr), (ct, dr))[k]
        pltpu.make_async_copy(src.at[pl.ds(t * HIST, HIST)], dst.at[t], loc.at[4 + k]).start()
        for i in range(1, HEADS):
            q = lax.rem(t + i, HEADS)
            remote(src.at[pl.ds(q * HIST, HIST)], dst.at[t], a2a_send.at[k], a2a_recv.at[k], (u, q)).start()

    pieces = (w_in.at[:, pl.ds(0, 384)], w_in.at[:, pl.ds(384, 128)], w_out)
    slots = (
        gz.at[c, mine, z, y * 2 + x_lo],
        gx.at[c, mine, x, (y // 2) * NZ + z],
        gy.at[c, mine, y, x_lo * NZ + z],
    )
    own = [pltpu.make_async_copy(pieces[k], slots[k], loc.at[k]) for k in range(3)]
    own.append(pltpu.make_async_copy(tab, tabs.at[c, x_lo, z], loc.at[3]))
    for copy in own:
        copy.start()
    for i in range(1, NX):
        remote(pieces[0], slots[0], st1_send.at[0], st1_recv.at[0], device_of(x_peer(i), y, z, c)).start()
    for i in range(1, NZ):
        device = device_of(x, y, z_peer(i), c)
        for col in (1, 2):
            remote(pieces[col], slots[col], st1_send.at[col], st1_recv.at[col], device).start()
    for i in range(1, NZ):
        remote(tab, tabs.at[c, x_lo, z], tab_send.at[0], tab_recv.at[0], device_of(x, y, z_peer(i), c)).start()
    for copy in own:
        copy.wait()

    def line_z(g):
        line = gz.at[c, g, z, pl.ds(y * 2, 2)]
        for i in range(1, NY):
            remote(line, line, z2_send.at[g], z2_recv.at[g], device_of(x, y_peer(i), z, c)).start()

    wait_bytes(gz.at[c, 0, z, pl.ds(0, NX - 1)], st1_recv.at[0])
    line_z(0)
    line_z(1)
    line_x = gx.at[c, mine, x, pl.ds((y // 2) * NZ, NZ)]
    line_y = gy.at[c, mine, y, pl.ds(x_lo * NZ, NZ)]
    wait_bytes(gx.at[c, mine, x, pl.ds(0, NZ - 1)], st1_recv.at[1])
    for i in range(1, NY):
        remote(line_x, line_x, st2_send.at[1], x2_recv.at[y], device_of(x, y_peer(i), z, c)).start()
    wait_bytes(gy.at[c, mine, y, pl.ds(0, NZ - 1)], st1_recv.at[2])
    for i in range(1, NX):
        remote(line_y, line_y, st2_send.at[2], y2_recv.at[x], device_of(x_peer(i), y, z, c)).start()

    wait_bytes(tabs.at[c, x_lo, pl.ds(0, NZ - 1)], tab_recv.at[0])
    rows_tab = tabs.at[c, x_lo]
    remote(rows_tab, rows_tab, tab_send.at[1], tab_recv.at[1], device_of(x + 1 - 2 * x_lo, y, z, c)).start()

    def half_of(ref, half):
        return ref.at[pl.ds(half * (ZM // 2), ZM // 2)]

    def ring_sem(g, k, direction, half):
        return g * 16 + (direction * (NZ // 2) + k) * 2 + half

    def block(g, idx, half):
        return half_of(gz.at[c, g, idx], half)

    def forward(col, g, part):
        remote(part, part, fw_send.at[g * 3 + col], fw_recv.at[g * 3 + col], partner).start()

    def ring_part(g, k, direction, half):
        step = 1 - 2 * direction
        part = block(g, lax.rem(z - step * k + NZ, NZ), half)
        s = ring_sem(g, k, direction, half)
        remote(part, part, ag_send.at[s], ag_recv.at[s], z_device(step)).start()

    def last_sem(g, col, q):
        return (g * 2 + col - 1) * 4 + q

    def ag_start_z(g):
        wait_bytes(gz.at[c, g, z, pl.ds(0, 6)], z2_recv.at[g])
        for half in (0, 1):
            for direction in (0, 1):
                ring_part(g, 0, direction, half)
        forward(0, g, gz.at[c, g, z])

    def ag_start_xy(g):
        for yy in range(2):
            src = yy * 2 + lax.rem(g + x_hi, 2)
            pl.when(src != y)(lambda: wait_bytes(gx.at[c, g, x, pl.ds(yy * NZ, NZ)], x2_recv.at[src]))
        for xl in range(2):
            src = lax.rem(g + y, 2) * 2 + xl
            pl.when(src != x)(lambda: wait_bytes(gy.at[c, g, y, pl.ds(xl * NZ, NZ)], y2_recv.at[src]))
        for col in (1, 2):
            part = gs[col].at[c, g, place[col]]
            for i in (1, 3, 2):
                s = last_sem(g, col, place[col])
                remote(part, part, last_send.at[g * 2 + col - 1], last_recv.at[s], last_peer(col, i)[1]).start()
            forward(col, g, part)

    def ag_take_xy(g):
        for i in (1, 3, 2):
            for col in (1, 2):
                q = last_peer(col, i)[0]
                part = gs[col].at[c, g, q]
                wait_bytes(part, last_recv.at[last_sem(g, col, q)])
                forward(col, g, part)

    def ag_step(g, k):
        last = NZ // 2 - 1

        def part_step(half, direction):
            step = 1 - 2 * direction
            idx = lax.rem(z - step * (k + 1) + NZ, NZ)
            wait_bytes(block(g, idx, half), ag_recv.at[ring_sem(g, k, direction, half)])
            more = k + 1 <= last if half == direction else k + 1 < last
            when(more, lambda: ring_part(g, k + 1, direction, half))
            forward(0, g, block(g, idx, half))

        for half in (0, 1):
            for direction in (0, 1):
                active = k <= last if half == direction else k < last
                when(active, lambda: part_step(half, direction))

    def ag_done(g):
        for col in range(3):
            wait_bytes(gs[col].at[1 - c, g], fw_recv.at[g * 3 + col])

    def norm_rows():
        pltpu.make_async_copy(xr.at[t], xr.at[t], loc.at[4]).wait()
        wait_bytes(xr.at[pl.ds(0, HEADS - 1)], a2a_recv.at[0])
        for i in range(HIST):
            rows = pl.ds(i * SEQ, SEQ)
            xs = jnp.concatenate([xr[k, i] for k in range(HEADS)], axis=1).astype(F32)
            cen = xs - jnp.mean(xs, axis=1, keepdims=True)
            rstd = lax.rsqrt(jnp.mean(cen * cen, axis=1, keepdims=True) + EPS)
            nfi = cen * rstd
            nf[rows, :] = nfi
            rstd_s[rows, :] = jnp.broadcast_to(rstd, (SEQ, 128))
            nbi = nfi.astype(BF16)
            nb[rows, :] = nbi
            nbt[:, rows] = nbi.T

    def mask_rows():
        pltpu.make_async_copy(dr.at[t], dr.at[t], loc.at[5]).wait()
        wait_bytes(dr.at[pl.ds(0, HEADS - 1)], a2a_recv.at[1])
        wait_bytes(tabs.at[1 - c], tab_recv.at[2])
        lens = jnp.zeros((1, 128), F32)
        for cc in range(2):
            for xl in range(2):
                rows = tabs[cc, xl]
                lens = lens + jnp.sum(
                    jnp.where(rows[:, 0, :] == u, rows[:, 1, :], 0).astype(F32), axis=0, keepdims=True
                )
        lane = lax.broadcasted_iota(jnp.int32, (1, 128), 1)
        pos = lax.broadcasted_iota(jnp.int32, (SEQ, D), 0).astype(F32)
        for i in range(HIST):
            rows = pl.ds(i * SEQ, SEQ)
            length = jnp.sum(jnp.where(lane == t * HIST + i, lens, 0.0), axis=1, keepdims=True)
            di = jnp.concatenate([dr[k, i] for k in range(HEADS)], axis=1).astype(F32)
            di = jnp.where(pos < length, di, 0.0).astype(BF16)
            dm[rows, :] = di
            dmt[:, rows] = di.T
        dn[...] = jnp.zeros_like(dn)

    scale = HD ** (-0.5)
    hs = [slice(i * SEQ, i * SEQ + SEQ) for i in range(HIST)]
    causal_one = lax.broadcasted_iota(jnp.int32, (SEQ, SEQ), 1) <= lax.broadcasted_iota(jnp.int32, (SEQ, SEQ), 0)

    def each(f):
        return jnp.concatenate([f(r) for r in hs], axis=0)

    def attention(zv, grad_h, k):
        gv, sg = silu_parts(zv)
        gv = gv.astype(BF16)
        uf = gv[:, 0:128].astype(F32)
        vp, qp, kp = gv[:, 128:256], gv[:, 256:384], gv[:, 384:512]
        yield
        s = each(lambda r: dot(qp[r], kp[r], NT)) * scale
        causal = jnp.concatenate([causal_one] * HIST, axis=0)
        ss, sgs = silu_parts(s)
        at = jnp.where(causal, ss / SEQ, 0.0).astype(BF16)
        yield
        yv = each(lambda r: dot(at[r], vp[r], NN))
        ycen = yv - jnp.mean(yv, axis=1, keepdims=True)
        yield
        yrstd = lax.rsqrt(jnp.mean(ycen * ycen, axis=1, keepdims=True) + EPS)
        yn = ycen * yrstd
        hb_s[:, k * 128 : k * 128 + 128] = (yn * uf).astype(BF16)
        dz_s[:, k * 512 : k * 512 + 128] = (grad_h * yn * sg[:, 0:128]).astype(BF16)
        yield
        gyn = grad_h * uf
        dy = (
            (gyn - jnp.mean(gyn, axis=1, keepdims=True) - yn * jnp.mean(gyn * yn, axis=1, keepdims=True)) * yrstd
        ).astype(BF16)
        yield
        da = each(lambda r: dot(dy[r], vp[r], NT))
        dz_s[:, k * 512 + 128 : k * 512 + 256] = (each(lambda r: dot(at[r], dy[r], TN)) * sg[:, 128:256]).astype(BF16)
        yield
        ds_ = jnp.where(causal, da * sgs * (scale / SEQ), 0.0).astype(BF16)
        yield
        dz_s[:, k * 512 + 256 : k * 512 + 384] = (each(lambda r: dot(ds_[r], kp[r], NN)) * sg[:, 256:384]).astype(BF16)
        dz_s[:, k * 512 + 384 : k * 512 + 512] = (each(lambda r: dot(ds_[r], qp[r], TN)) * sg[:, 384:512]).astype(BF16)

    def beside(stages, others):
        others = list(others)
        for _ in stages:
            if others:
                others.pop(0)()
        for other in others:
            other()

    def pair(g, yy, middle):
        for k in range(2):
            hy = 2 * yy + k
            hx = lax.rem(g + hy, 2)
            for xl in range(2):
                for zz in range(NZ):
                    for cc in range(2):
                        r = pl.ds(((xl * NZ + zz) * 2 + cc) * 32, 32)
                        wh[r, pl.ds(k * 512, 384)] = gz[cc, g, zz, hy * 2 + xl]
                        wh[r, pl.ds(k * 512 + 384, 128)] = gx[cc, g, hx * 2 + xl, yy * NZ + zz]
                        wo[r, pl.ds(k * 128, 128)] = gy[cc, g, hy, xl * NZ + zz]

        def z_rows(i):
            def run():
                rows = pl.ds(i * 64, 64)
                z_s[rows, :] = dot(nb[rows, :], wh[:, 512:1024], NN)

            return run

        def out_of(k, j):
            hy = 2 * yy + k
            hx = lax.rem(g + hy, 2)

            def weights():
                gw = dot(nbt[pl.ds(j * 256, 256), :], dz_s[:, k * 512 : k * 512 + 512], NN).astype(BF16)
                for i in range(8):
                    uu = j * 8 + i
                    cc, zz, xl = uu % 2, (uu // 2) % NZ, uu // (2 * NZ)
                    pz[cc, g, zz, hy * 2 + xl] = gw[i * 32 : i * 32 + 32, 0:384]
                    px[cc, g, hx * 2 + xl, yy * NZ + zz] = gw[i * 32 : i * 32 + 32, 384:512]

            def rows():
                dn[:, pl.ds(j * 256, 256)] += dot(
                    dz_s[:, k * 512 : k * 512 + 512], wh[pl.ds(j * 256, 256), k * 512 : k * 512 + 512], NT
                )

            return [weights, rows]

        def both(j):
            def run():
                go = dot(dmt[pl.ds(j * 256, 256), :], hb_s[...], NN).astype(BF16)
                for i in range(8):
                    uu = j * 8 + i
                    cc, zz, xl = uu % 2, (uu // 2) % NZ, uu // (2 * NZ)
                    for k in range(2):
                        py[cc, g, 2 * yy + k, xl * NZ + zz] = go[i * 32 : i * 32 + 32, k * 128 : k * 128 + 128]

            return run

        z0 = dot(nb[...], wh[:, 0:512], NN)
        grad_h = dot(dm[...], wo[...], NN)
        beside(attention(z0, grad_h[:, 0:128], 0), [z_rows(i) for i in range(8)])
        middle()
        first = [f for j in range(4) for f in out_of(0, j)]
        beside(attention(z_s[...], grad_h[:, 128:256], 1), first)
        for j in range(4):
            both(j)()
            for f in out_of(1, j):
                f()

    def rows_out():
        for i in range(HIST):
            rows = pl.ds(i * SEQ, SEQ)
            dni, nfi = dn[rows, :], nf[rows, :]
            branch = (
                dni - jnp.mean(dni, axis=1, keepdims=True) - nfi * jnp.mean(dni * nfi, axis=1, keepdims=True)
            ) * rstd_s[rows, 0:1]
            out = (dm[rows, :].astype(F32) + branch).astype(BF16)
            for k in range(HEADS):
                dr[k, i] = out[:, k * 128 : k * 128 + 128]

    def head_parts(ref_of, g, hy):
        hx = lax.rem(g + hy, 2)
        return (
            ref_of(0).at[:, pl.ds(hy * 2, 2)],
            ref_of(1).at[pl.ds(hx * 2, 2), pl.ds((hy // 2) * NZ, NZ)],
            ref_of(2).at[hy],
        )

    def to_partner(g, hy):
        src = head_parts(lambda col: ps[col].at[1 - c, g], g, hy)
        dst = head_parts(lambda col: ts[col].at[g], g, hy)
        for col in range(3):
            s = (g * 3 + col) * 4 + hy
            remote(src[col], dst[col], par_send.at[s], par_recv.at[s], partner).start()

    def from_partner(part):
        g = part // 2
        for hy in (part % 2 * 2, part % 2 * 2 + 1):
            dst = head_parts(lambda col: ts[col].at[g], g, hy)
            for col in range(3):
                wait_bytes(dst[col], par_recv.at[(g * 3 + col) * 4 + hy])

    def add_parts(own_part, parts, count):
        step = min(count, 4 if own_part.shape[-1] == 128 else 2)

        @pl.loop(0, count // step)
        def _(i):
            rows = pl.ds(i * step, step)
            v = own_part[rows].astype(F32)
            for ref in parts:
                v = v + ref[rows].astype(F32)
            own_part[rows] = v.astype(BF16)

    def rz_half(ref, yy, half):
        return ref.at[pl.ds(yy * 4 + half * 2, 2)]

    def rs_sem(part, k, direction, half):
        return part * 16 + (direction * (NZ // 2) + k) * 2 + half

    def rs_add(part, off, half, from_ring):
        g, yy = part // 2, part % 2
        idx = lax.rem(z + off + NZ, NZ)
        parts = [rz_half(tz.at[g, idx], yy, half)]
        for k, direction in from_ring:
            s = rs_sem(part, k, direction, half)
            wait_bytes(rz.at[s], rs_recv.at[s])
            parts.append(rz.at[s])
        add_parts(rz_half(pz.at[c, g, idx], yy, half), parts, 2)

    def rs_step(part, k):
        g, yy = part // 2, part % 2
        for half in (0, 1):
            for direction in (0, 1):
                if k == 0 and half != direction:
                    continue
                off = NZ // 2 - k if direction == 0 else k - NZ // 2
                rs_add(part, off, half, ((k - 1, direction),) if k > 1 or (k == 1 and half == direction) else ())
                s = rs_sem(part, k, direction, half)
                remote(
                    rz_half(pz.at[c, g, lax.rem(z + off + NZ, NZ)], yy, half), rz.at[s],
                    rs_send.at[s], rs_recv.at[s], z_device(1 - 2 * direction),
                ).start()

    def send_x(part):
        g, yy = part // 2, part % 2
        sub = pl.ds(yy * NZ, NZ)
        for i in (2, 1, 3):
            q, device = last_peer(1, i)
            add_parts(px.at[c, g, q, sub], [tx.at[g, q, sub]], NZ)
            remote(
                px.at[c, g, q, sub], rx.at[g, x, sub], rl_send.at[part], rl_recv.at[part * 4 + x], device
            ).start()

    def send_y(g):
        for i in (2, 1, 3):
            q, device = last_peer(2, i)
            add_parts(py.at[c, g, q], [ty.at[g, q]], 16)
            remote(
                py.at[c, g, q], ry.at[g, y], rl_send.at[4 + g], rl_recv.at[16 + g * 4 + y], device
            ).start()

    def take_x(part):
        g, yy = part // 2, part % 2
        sub = pl.ds(yy * NZ, NZ)
        parts = [tx.at[g, x, sub]]
        for i in (1, 3, 2):
            q = x_peer(i)
            wait_bytes(rx.at[g, q, sub], rl_recv.at[part * 4 + q])
            parts.append(rx.at[g, q, sub])
        add_parts(px.at[c, g, x, sub], parts, NZ)
        for i in range(1, NY):
            q = y_peer(i)
            device = device_of(x, q, z, c)

            @pl.when((lax.rem(q + x_hi, 2) == g) & (q // 2 == yy))
            def _():
                remote(px.at[c, g, x, sub], s1x.at[y], o1_send.at[0], o1_recv.at[0], device).start()

    def take_y(g):
        parts = [ty.at[g, y]]
        for i in (1, 3, 2):
            q = y_peer(i)
            wait_bytes(ry.at[g, q], rl_recv.at[16 + g * 4 + q])
            parts.append(ry.at[g, q])
        add_parts(py.at[c, g, y], parts, 16)
        for i in range(1, NX):
            q = x_peer(i)
            device = device_of(q, y, z, c)

            @pl.when(lax.rem(y + q // 2, 2) == g)
            def _():
                remote(
                    py.at[c, g, y, pl.ds(lax.rem(q, 2) * NZ, NZ)], s1y.at[x], o1_send.at[1], o1_recv.at[1], device
                ).start()

    def take_z(part):
        g, yy = part // 2, part % 2
        for half in (0, 1):
            rs_add(part, 0, half, tuple((NZ // 2 - 1, d) for d in (0, 1)))
        for i in range(1, NY):
            q = y_peer(i)
            device = device_of(x, q, z, c)

            @pl.when(q // 2 == yy)
            def _():
                remote(
                    pz.at[c, g, z, pl.ds(q * 2, 2)], s1z.at[g, y], o1z_send.at[g], o1z_recv.at[g], device
                ).start()

    ag_start_z(0)
    ag_start_z(1)
    ag_start_xy(0)
    send_rows(0)
    send_rows(1)
    ag_step(0, 0)
    wait_bytes(tabs.at[c, 1 - x_lo], tab_recv.at[1])
    remote(tabs.at[c], tabs.at[c], tab_send.at[2], tab_recv.at[2], partner).start()
    ag_step(1, 0)
    ag_start_xy(1)
    ag_step(0, 1)
    ag_step(1, 1)
    ag_step(0, 2)
    ag_step(1, 2)
    ag_take_xy(0)
    norm_rows()
    ag_step(0, 3)
    ag_step(1, 3)
    mask_rows()
    ag_done(0)

    @pl.loop(0, 2)
    def _(j):
        def middle():
            @pl.when(j == 0)
            def _():
                ag_take_xy(1)

            @pl.when(j == 1)
            def _():
                from_partner(0)
                rs_step(0, 0)
                send_x(0)

        pair(0, j, middle)
        to_partner(0, 2 * j)
        to_partner(0, 2 * j + 1)
        pl.when(j == 1)(lambda: rs_step(0, 1))

    ag_done(1)

    @pl.loop(0, 2)
    def _(j):
        def middle():
            @pl.when(j == 0)
            def _():
                rs_step(0, 2)
                from_partner(1)
                rs_step(1, 0)
                send_x(1)
                send_y(0)

            @pl.when(j == 1)
            def _():
                rs_step(1, 2)
                from_partner(2)
                rs_step(2, 0)
                send_x(2)
                take_z(0)
                take_x(0)

        pair(1, j, middle)
        to_partner(1, 2 * j)
        to_partner(1, 2 * j + 1)

        @pl.when(j == 0)
        def _():
            rs_step(0, 3)
            rs_step(1, 1)

        @pl.when(j == 1)
        def _():
            rs_step(1, 3)
            rs_step(2, 1)

    rows_out()
    for i in range(1, HEADS):
        q = lax.rem(t + i, HEADS)
        remote(dr.at[q], grad_x.at[pl.ds(t * HIST, HIST)], out_send, out_recv, (u, q)).start()
    pltpu.make_async_copy(dr.at[t], grad_x.at[pl.ds(t * HIST, HIST)], loc.at[6]).start()
    from_partner(3)
    rs_step(3, 0)
    send_x(3)
    send_y(1)
    rs_step(2, 2)
    take_z(1)
    take_x(1)
    take_y(0)
    rs_step(3, 1)
    rs_step(2, 3)
    rs_step(3, 2)
    take_z(2)
    take_x(2)
    rs_step(3, 3)
    take_x(3)
    take_y(1)
    take_z(3)

    wait_bytes(s1x.at[pl.ds(0, NY - 1)], o1_recv.at[0])
    line_px = px.at[c, mine, x, pl.ds((y // 2) * NZ, NZ)]
    add_parts(line_px, [s1x.at[y_peer(i)] for i in range(1, NY)], NZ)
    for i in range(1, NZ):
        q = z_peer(i)
        remote(line_px.at[q], s2x.at[z], o2_send.at[1], o2_recv.at[1], device_of(x, y, q, c)).start()
    wait_bytes(s1y.at[pl.ds(0, NX - 1)], o1_recv.at[1])
    line_py = py.at[c, mine, y, pl.ds(x_lo * NZ, NZ)]
    add_parts(line_py, [s1y.at[x_peer(i)] for i in range(1, NX)], NZ)
    for i in range(1, NZ):
        q = z_peer(i)
        remote(line_py.at[q], s2y.at[z], o2_send.at[2], o2_recv.at[2], device_of(x, y, q, c)).start()
    for g in range(2):
        wait_bytes(s1z.at[g, pl.ds(0, NY - 1)], o1z_recv.at[g])
        add_parts(pz.at[c, g, z, pl.ds(y * 2, 2)], [s1z.at[g, y_peer(i)] for i in range(1, NY)], 2)
    for i in range(1, NX):
        q = x_peer(i)
        remote(
            pz.at[c, lax.rem(y + q // 2, 2), z, y * 2 + lax.rem(q, 2)], s2z.at[x], o2_send.at[0], o2_recv.at[0],
            device_of(q, y, z, c),
        ).start()

    wait_bytes(s2x.at[pl.ds(0, NZ - 1)], o2_recv.at[1])
    total = line_px[z].astype(F32)
    for i in range(1, NZ):
        total = total + s2x[z_peer(i)].astype(F32)
    grad_wi[:, pl.ds(384, 128)] = total
    wait_bytes(s2y.at[pl.ds(0, NZ - 1)], o2_recv.at[2])
    total = line_py[z].astype(F32)
    for i in range(1, NZ):
        total = total + s2y[z_peer(i)].astype(F32)
    grad_wo[...] = total
    wait_bytes(s2z.at[pl.ds(0, NX - 1)], o2_recv.at[0])
    total = pz[c, mine, z, y * 2 + x_lo].astype(F32)
    for i in range(1, NX):
        total = total + s2z[x_peer(i)].astype(F32)
    grad_wi[:, pl.ds(0, 384)] = total

    wait_bytes(gx.at[c, mine, x, pl.ds(0, NZ - 1)], st1_send.at[1])
    wait_bytes(gy.at[c, mine, y, pl.ds(0, NZ - 1)], st1_send.at[2])
    wait_bytes(gz.at[c, 0, z, pl.ds(0, NX - 1)], st1_send.at[0])
    wait_bytes(s1x.at[pl.ds(0, NY - 1)], st2_send.at[1])
    wait_bytes(s1y.at[pl.ds(0, NX - 1)], st2_send.at[2])
    for g in range(2):
        wait_bytes(gz.at[c, g, z, pl.ds(0, 6)], z2_send.at[g])
        wait_bytes(s1z.at[g, pl.ds(0, NY - 1)], o1z_send.at[g])
    wait_bytes(tabs.at[c, x_lo, pl.ds(0, NZ - 1)], tab_send.at[0])
    wait_bytes(tabs.at[c, x_lo], tab_send.at[1])
    wait_bytes(tabs.at[c], tab_send.at[2])
    wait_bytes(s1x.at[pl.ds(0, NY - 1)], o1_send.at[0])
    wait_bytes(s1y.at[pl.ds(0, NX - 1)], o1_send.at[1])
    wait_bytes(s2z.at[pl.ds(0, NX - 1)], o2_send.at[0])
    wait_bytes(s2x.at[pl.ds(0, NZ - 1)], o2_send.at[1])
    wait_bytes(s2y.at[pl.ds(0, NZ - 1)], o2_send.at[2])
    for k, ref in enumerate((xr, dr)):
        wait_bytes(ref.at[pl.ds(0, HEADS - 1)], a2a_send.at[k])
    for g in range(2):
        for col in range(3):
            wait_bytes(gs[col].at[c, g], fw_send.at[g * 3 + col])
            for hy in range(NY):
                dst = head_parts(lambda k: ts[k].at[g], g, hy)
                wait_bytes(dst[col], par_send.at[(g * 3 + col) * 4 + hy])
        for col in (1, 2):
            wait_bytes(rings[col].at[g, pl.ds(0, 3)], last_send.at[g * 2 + col - 1])
        for half in (0, 1):
            for direction in (0, 1):
                for k in range(NZ // 2):
                    s = ring_sem(g, k, direction, half)
                    if half == direction or k < NZ // 2 - 1:
                        wait_bytes(block(g, 0, half), ag_send.at[s])
                    if half == direction or k > 0:
                        for part in (2 * g, 2 * g + 1):
                            s = rs_sem(part, k, direction, half)
                            wait_bytes(rz.at[s], rs_send.at[s])
        wait_bytes(ry.at[g, pl.ds(0, 3)], rl_send.at[4 + g])
        for part in (2 * g, 2 * g + 1):
            wait_bytes(rx.at[g, pl.ds(0, 3), pl.ds(0, NZ)], rl_send.at[part])
    pltpu.make_async_copy(dr.at[t], grad_x.at[pl.ds(t * HIST, HIST)], loc.at[6]).wait()
    wait_bytes(dr.at[pl.ds(0, HEADS - 1)], out_send)
    wait_bytes(dr.at[pl.ds(0, HEADS - 1)], out_recv)


def local(events, cotangent, w_in, w_out, slot_source, slot_length):
    tab = jnp.pad(jnp.stack([slot_source, slot_length]), ((0, 6), (0, 96)))
    any_ = pl.BlockSpec(memory_space=pl.ANY)
    vmem = pl.BlockSpec(memory_space=pltpu.VMEM)
    shape = jax.ShapeDtypeStruct
    dma = pltpu.SemaphoreType.DMA
    both = [pltpu.VMEM((2, 2, n, m, 32, w), BF16) for _, n, m, w in COLOURS]
    theirs = [pltpu.VMEM((2, n, m, 32, w), BF16) for _, n, m, w in COLOURS]
    rings = [pltpu.VMEM((64, 2, 32, 384), BF16)] + [pltpu.VMEM((2, n, m, 32, w), BF16) for _, n, m, w in COLOURS[1:]]
    lines = [
        pltpu.VMEM((2, NY, 2, 32, 384), BF16),
        pltpu.VMEM((NY, NZ, 32, 128), BF16),
        pltpu.VMEM((NX, NZ, 32, 128), BF16),
        pltpu.VMEM((NX, 32, 384), BF16),
        pltpu.VMEM((NZ, 32, 128), BF16),
        pltpu.VMEM((NZ, 32, 128), BF16),
    ]
    work = [
        pltpu.VMEM((HEADS, HIST, SEQ, 128), BF16),
        pltpu.VMEM((HEADS, HIST, SEQ, 128), BF16),
        pltpu.VMEM((2, 2, NZ, 8, 128), jnp.int32),
        pltpu.VMEM((ROWS, D), F32),
        pltpu.VMEM((ROWS, D), BF16),
        pltpu.VMEM((D, ROWS), BF16),
        pltpu.VMEM((ROWS, D), BF16),
        pltpu.VMEM((D, ROWS), BF16),
        pltpu.VMEM((ROWS, 128), F32),
        pltpu.VMEM((ROWS, D), F32),
        pltpu.VMEM((D, 1024), BF16),
        pltpu.VMEM((D, 256), BF16),
        pltpu.VMEM((ROWS, 1024), BF16),
        pltpu.VMEM((ROWS, 256), BF16),
        pltpu.VMEM((ROWS, 512), F32),
    ]
    sems = [
        dma((7,)), dma((3,)), dma((3,)), dma((3,)), dma((2,)), dma((2,)), dma((NY,)), dma((NX,)),
        dma((32,)), dma((32,)), dma((6,)), dma((6,)), dma((2,)), dma((2,)), dma((3,)), dma((3,)),
        dma((24,)), dma((24,)), dma((64,)), dma((64,)), dma((4,)), dma((16,)), dma((6,)), dma((24,)),
        dma((2,)), dma((2,)), dma((2,)), dma((2,)), dma((3,)), dma((3,)), dma, dma,
    ]
    return pl.pallas_call(
        kernel,
        out_shape=(shape((32, SEQ, 128), BF16), shape((32, 512), F32), shape((32, 128), F32)),
        in_specs=[any_, any_, vmem, vmem, vmem],
        out_specs=(any_, vmem, vmem),
        scratch_shapes=both + both + theirs + rings + lines + work + sems,
        compiler_params=pltpu.CompilerParams(
            has_side_effects=True, collective_id=0, vmem_limit_bytes=64 * 1024 * 1024 - 131072
        ),
        name="step",
    )(events, cotangent, w_in, w_out, tab)


def solution(mesh):
    in_specs = (
        P("user", None, "tensor"),
        P("user", None, "tensor"),
        P("user", "tensor"),
        P("user", "tensor"),
        P("user"),
        P("user"),
    )
    out_specs = (P("user", None, "tensor"), P("user", "tensor"), P("user", "tensor"))
    return jax.shard_map(local, mesh=mesh, in_specs=in_specs, out_specs=out_specs, check_vma=False)
```

```python
import jax
import jax.numpy as jnp
from jax import lax
from jax.experimental import pallas as pl
from jax.experimental.pallas import tpu as pltpu
from jax.sharding import PartitionSpec as P

MESH = pl.DeviceIdType.MESH
F32 = jnp.float32
BF16 = jnp.bfloat16
EPS = 1e-05
HD = 128
SEQ = 128
HEADS = 8
NX, NY, NZ = 4, 4, 8
HIST = 4
ROWS = HIST * SEQ
D = 1024

COLOURS = ((2, NZ, 8, 384), (0, NX, 16, 128), (1, NY, 16, 128))
ZM = 8


def device_of(x, y, z, c):
    return ((lax.rem(x, 2) * NZ + z) * 2 + c, y * 2 + x // 2)


def remote(src, dst, send, recv, device):
    return pltpu.make_async_remote_copy(
        src_ref=src, dst_ref=dst, send_sem=send, recv_sem=recv, device_id=device, device_id_type=MESH
    )


def wait_bytes(ref, sem):
    pltpu.make_async_copy(ref, ref, sem).wait()


def silu_parts(v):
    sig = jax.nn.sigmoid(v)
    return v * sig, sig * (1.0 + v * (1.0 - sig))


def dot(a, b, dims):
    return lax.dot_general(a, b, (dims, ((), ())), preferred_element_type=F32)


NN, NT, TN = ((1,), (0,)), ((1,), (1,)), ((0,), (0,))


def when(cond, f):
    if isinstance(cond, bool):
        if cond:
            f()
    else:
        pl.when(cond)(f)


def kernel(
    ev, ct, w_in, w_out, tab, grad_x, grad_wi, grad_wo,
    gz, gx, gy, pz, px, py, tz, tx, ty, rz, rx, ry, s1z, s1x, s1y, s2z, s2x, s2y,
    xr, dr, tabs, nf, nb, nbt, dm, dmt, rstd_s, dn, wh, wo, dz_s, hb_s, z_s,
    loc, st1_send, st1_recv, st2_send, z2_send, z2_recv, x2_recv, y2_recv, ag_send, ag_recv, fw_send, fw_recv,
    a2a_send, a2a_recv, tab_send, tab_recv, par_send, par_recv, rs_send, rs_recv,
    last_send, last_recv, rl_send, rl_recv,
    o1_send, o1z_send, o1_recv, o1z_recv, o2_send, o2_recv, out_send, out_recv,
):
    u = lax.axis_index("user")
    t = lax.axis_index("tensor")
    c = lax.rem(u, 2)
    z = lax.rem(u // 2, NZ)
    x_lo = u // (2 * NZ)
    x_hi = lax.rem(t, 2)
    y = t // 2
    x = x_hi * 2 + x_lo
    mine = lax.rem(y + x_hi, 2)
    partner = (u + 1 - 2 * c, t)
    gs, ps, ts, rings = (gz, gx, gy), (pz, px, py), (tz, tx, ty), (rz, rx, ry)
    place = (z, x, y)

    def x_peer(i):
        return lax.rem(x + i, NX)

    def y_peer(i):
        return lax.rem(y + i, NY)

    def z_peer(i):
        return lax.rem(z + i, NZ)

    def z_device(step):
        return device_of(x, y, lax.rem(z + step + NZ, NZ), c)

    def last_peer(col, i):
        q = x_peer(i) if col == 1 else y_peer(i)
        return q, device_of(q, y, z, c) if col == 1 else device_of(x, q, z, c)

    barrier = pltpu.get_barrier_semaphore()

    def greet(device):
        pl.semaphore_signal(barrier, inc=1, device_id=device, device_id_type=MESH)

    greet(partner)
    for i in range(1, NX):
        greet(device_of(x_peer(i), y, z, c))
    for i in range(1, NY):
        greet(device_of(x, y_peer(i), z, c))
        greet((u, y_peer(i) * 2 + 1 - x_hi))
    for i in range(1, NZ):
        greet(device_of(x, y, z_peer(i), c))
    pl.semaphore_wait(barrier, 17)

    def send_rows(k):
        src, dst = ((ev, xr), (ct, dr))[k]
        pltpu.make_async_copy(src.at[pl.ds(t * HIST, HIST)], dst.at[t], loc.at[4 + k]).start()
        for i in range(1, HEADS):
            q = lax.rem(t + i, HEADS)
            remote(src.at[pl.ds(q * HIST, HIST)], dst.at[t], a2a_send.at[k], a2a_recv.at[k], (u, q)).start()

    pieces = (w_in.at[:, pl.ds(0, 384)], w_in.at[:, pl.ds(384, 128)], w_out)
    slots = (
        gz.at[c, mine, z, y * 2 + x_lo],
        gx.at[c, mine, x, (y // 2) * NZ + z],
        gy.at[c, mine, y, x_lo * NZ + z],
    )
    own = [pltpu.make_async_copy(pieces[k], slots[k], loc.at[k]) for k in range(3)]
    own.append(pltpu.make_async_copy(tab, tabs.at[c, x_lo, z], loc.at[3]))
    for copy in own:
        copy.start()
    for i in range(1, NX):
        remote(pieces[0], slots[0], st1_send.at[0], st1_recv.at[0], device_of(x_peer(i), y, z, c)).start()
    for i in range(1, NZ):
        device = device_of(x, y, z_peer(i), c)
        for col in (1, 2):
            remote(pieces[col], slots[col], st1_send.at[col], st1_recv.at[col], device).start()
    for i in range(1, NZ):
        remote(tab, tabs.at[c, x_lo, z], tab_send.at[0], tab_recv.at[0], device_of(x, y, z_peer(i), c)).start()
    for copy in own:
        copy.wait()

    def line_z(g):
        line = gz.at[c, g, z, pl.ds(y * 2, 2)]
        for i in range(1, NY):
            remote(line, line, z2_send.at[g], z2_recv.at[g], device_of(x, y_peer(i), z, c)).start()

    wait_bytes(gz.at[c, 0, z, pl.ds(0, NX - 1)], st1_recv.at[0])
    line_z(0)
    line_z(1)
    line_x = gx.at[c, mine, x, pl.ds((y // 2) * NZ, NZ)]
    line_y = gy.at[c, mine, y, pl.ds(x_lo * NZ, NZ)]
    wait_bytes(gx.at[c, mine, x, pl.ds(0, NZ - 1)], st1_recv.at[1])
    for i in range(1, NY):
        remote(line_x, line_x, st2_send.at[1], x2_recv.at[y], device_of(x, y_peer(i), z, c)).start()
    wait_bytes(gy.at[c, mine, y, pl.ds(0, NZ - 1)], st1_recv.at[2])
    for i in range(1, NX):
        remote(line_y, line_y, st2_send.at[2], y2_recv.at[x], device_of(x_peer(i), y, z, c)).start()

    wait_bytes(tabs.at[c, x_lo, pl.ds(0, NZ - 1)], tab_recv.at[0])
    rows_tab = tabs.at[c, x_lo]
    remote(rows_tab, rows_tab, tab_send.at[1], tab_recv.at[1], device_of(x + 1 - 2 * x_lo, y, z, c)).start()

    def half_of(ref, half):
        return ref.at[pl.ds(half * (ZM // 2), ZM // 2)]

    def ring_sem(g, k, direction, half):
        return g * 16 + (direction * (NZ // 2) + k) * 2 + half

    def block(g, idx, half):
        return half_of(gz.at[c, g, idx], half)

    def forward(col, g, part):
        remote(part, part, fw_send.at[g * 3 + col], fw_recv.at[g * 3 + col], partner).start()

    def ring_part(g, k, direction, half):
        step = 1 - 2 * direction
        part = block(g, lax.rem(z - step * k + NZ, NZ), half)
        s = ring_sem(g, k, direction, half)
        remote(part, part, ag_send.at[s], ag_recv.at[s], z_device(step)).start()

    def last_sem(g, col, q):
        return (g * 2 + col - 1) * 4 + q

    def ag_start_z(g):
        wait_bytes(gz.at[c, g, z, pl.ds(0, 6)], z2_recv.at[g])
        for half in (0, 1):
            for direction in (0, 1):
                ring_part(g, 0, direction, half)
        forward(0, g, gz.at[c, g, z])

    def ag_start_xy(g):
        for yy in range(2):
            src = yy * 2 + lax.rem(g + x_hi, 2)
            pl.when(src != y)(lambda: wait_bytes(gx.at[c, g, x, pl.ds(yy * NZ, NZ)], x2_recv.at[src]))
        for xl in range(2):
            src = lax.rem(g + y, 2) * 2 + xl
            pl.when(src != x)(lambda: wait_bytes(gy.at[c, g, y, pl.ds(xl * NZ, NZ)], y2_recv.at[src]))
        for col in (1, 2):
            part = gs[col].at[c, g, place[col]]
            for i in (1, 3, 2):
                s = last_sem(g, col, place[col])
                remote(part, part, last_send.at[g * 2 + col - 1], last_recv.at[s], last_peer(col, i)[1]).start()
            forward(col, g, part)

    def ag_take_xy(g):
        for i in (1, 3, 2):
            for col in (1, 2):
                q = last_peer(col, i)[0]
                part = gs[col].at[c, g, q]
                wait_bytes(part, last_recv.at[last_sem(g, col, q)])
                forward(col, g, part)

    def ag_step(g, k):
        last = NZ // 2 - 1

        def part_step(half, direction):
            step = 1 - 2 * direction
            idx = lax.rem(z - step * (k + 1) + NZ, NZ)
            wait_bytes(block(g, idx, half), ag_recv.at[ring_sem(g, k, direction, half)])
            more = k + 1 <= last if half == direction else k + 1 < last
            when(more, lambda: ring_part(g, k + 1, direction, half))
            forward(0, g, block(g, idx, half))

        for half in (0, 1):
            for direction in (0, 1):
                active = k <= last if half == direction else k < last
                when(active, lambda: part_step(half, direction))

    def ag_done(g):
        for col in range(3):
            wait_bytes(gs[col].at[1 - c, g], fw_recv.at[g * 3 + col])

    def norm_rows():
        pltpu.make_async_copy(xr.at[t], xr.at[t], loc.at[4]).wait()
        wait_bytes(xr.at[pl.ds(0, HEADS - 1)], a2a_recv.at[0])
        for i in range(HIST):
            rows = pl.ds(i * SEQ, SEQ)
            xs = jnp.concatenate([xr[k, i] for k in range(HEADS)], axis=1).astype(F32)
            cen = xs - jnp.mean(xs, axis=1, keepdims=True)
            rstd = lax.rsqrt(jnp.mean(cen * cen, axis=1, keepdims=True) + EPS)
            nfi = cen * rstd
            nf[rows, :] = nfi
            rstd_s[rows, :] = jnp.broadcast_to(rstd, (SEQ, 128))
            nbi = nfi.astype(BF16)
            nb[rows, :] = nbi
            nbt[:, rows] = nbi.T

    def mask_rows():
        pltpu.make_async_copy(dr.at[t], dr.at[t], loc.at[5]).wait()
        wait_bytes(dr.at[pl.ds(0, HEADS - 1)], a2a_recv.at[1])
        wait_bytes(tabs.at[1 - c], tab_recv.at[2])
        lens = jnp.zeros((1, 128), F32)
        for cc in range(2):
            for xl in range(2):
                rows = tabs[cc, xl]
                lens = lens + jnp.sum(
                    jnp.where(rows[:, 0, :] == u, rows[:, 1, :], 0).astype(F32), axis=0, keepdims=True
                )
        lane = lax.broadcasted_iota(jnp.int32, (1, 128), 1)
        pos = lax.broadcasted_iota(jnp.int32, (SEQ, D), 0).astype(F32)
        for i in range(HIST):
            rows = pl.ds(i * SEQ, SEQ)
            length = jnp.sum(jnp.where(lane == t * HIST + i, lens, 0.0), axis=1, keepdims=True)
            di = jnp.concatenate([dr[k, i] for k in range(HEADS)], axis=1).astype(F32)
            di = jnp.where(pos < length, di, 0.0).astype(BF16)
            dm[rows, :] = di
            dmt[:, rows] = di.T
        dn[...] = jnp.zeros_like(dn)

    scale = HD ** (-0.5)
    hs = [slice(i * SEQ, i * SEQ + SEQ) for i in range(HIST)]
    causal_one = lax.broadcasted_iota(jnp.int32, (SEQ, SEQ), 1) <= lax.broadcasted_iota(jnp.int32, (SEQ, SEQ), 0)

    def each(f):
        return jnp.concatenate([f(r) for r in hs], axis=0)

    def attention(zv, grad_h, k):
        gv, sg = silu_parts(zv)
        gv = gv.astype(BF16)
        uf = gv[:, 0:128].astype(F32)
        vp, qp, kp = gv[:, 128:256], gv[:, 256:384], gv[:, 384:512]
        yield
        s = each(lambda r: dot(qp[r], kp[r], NT)) * scale
        causal = jnp.concatenate([causal_one] * HIST, axis=0)
        ss, sgs = silu_parts(s)
        at = jnp.where(causal, ss / SEQ, 0.0).astype(BF16)
        yield
        yv = each(lambda r: dot(at[r], vp[r], NN))
        ycen = yv - jnp.mean(yv, axis=1, keepdims=True)
        yield
        yrstd = lax.rsqrt(jnp.mean(ycen * ycen, axis=1, keepdims=True) + EPS)
        yn = ycen * yrstd
        hb_s[:, k * 128 : k * 128 + 128] = (yn * uf).astype(BF16)
        dz_s[:, k * 512 : k * 512 + 128] = (grad_h * yn * sg[:, 0:128]).astype(BF16)
        yield
        gyn = grad_h * uf
        dy = (
            (gyn - jnp.mean(gyn, axis=1, keepdims=True) - yn * jnp.mean(gyn * yn, axis=1, keepdims=True)) * yrstd
        ).astype(BF16)
        yield
        da = each(lambda r: dot(dy[r], vp[r], NT))
        dz_s[:, k * 512 + 128 : k * 512 + 256] = (each(lambda r: dot(at[r], dy[r], TN)) * sg[:, 128:256]).astype(BF16)
        yield
        ds_ = jnp.where(causal, da * sgs * (scale / SEQ), 0.0).astype(BF16)
        yield
        dz_s[:, k * 512 + 256 : k * 512 + 384] = (each(lambda r: dot(ds_[r], kp[r], NN)) * sg[:, 256:384]).astype(BF16)
        dz_s[:, k * 512 + 384 : k * 512 + 512] = (each(lambda r: dot(ds_[r], qp[r], TN)) * sg[:, 384:512]).astype(BF16)

    def beside(stages, others):
        others = list(others)
        for _ in stages:
            if others:
                others.pop(0)()
        for other in others:
            other()

    def pair(g, yy, middle):
        for k in range(2):
            hy = 2 * yy + k
            hx = lax.rem(g + hy, 2)
            for xl in range(2):
                for zz in range(NZ):
                    for cc in range(2):
                        r = pl.ds(((xl * NZ + zz) * 2 + cc) * 32, 32)
                        wh[r, pl.ds(k * 512, 384)] = gz[cc, g, zz, hy * 2 + xl]
                        wh[r, pl.ds(k * 512 + 384, 128)] = gx[cc, g, hx * 2 + xl, yy * NZ + zz]
                        wo[r, pl.ds(k * 128, 128)] = gy[cc, g, hy, xl * NZ + zz]

        def z_rows(i):
            def run():
                rows = pl.ds(i * 64, 64)
                z_s[rows, :] = dot(nb[rows, :], wh[:, 512:1024], NN)

            return run

        def out_of(k, j):
            hy = 2 * yy + k
            hx = lax.rem(g + hy, 2)

            def weights():
                gw = dot(nbt[pl.ds(j * 256, 256), :], dz_s[:, k * 512 : k * 512 + 512], NN).astype(BF16)
                for i in range(8):
                    uu = j * 8 + i
                    cc, zz, xl = uu % 2, (uu // 2) % NZ, uu // (2 * NZ)
                    pz[cc, g, zz, hy * 2 + xl] = gw[i * 32 : i * 32 + 32, 0:384]
                    px[cc, g, hx * 2 + xl, yy * NZ + zz] = gw[i * 32 : i * 32 + 32, 384:512]

            def rows():
                dn[:, pl.ds(j * 256, 256)] += dot(
                    dz_s[:, k * 512 : k * 512 + 512], wh[pl.ds(j * 256, 256), k * 512 : k * 512 + 512], NT
                )

            return [weights, rows]

        def both(j):
            def run():
                go = dot(dmt[pl.ds(j * 256, 256), :], hb_s[...], NN).astype(BF16)
                for i in range(8):
                    uu = j * 8 + i
                    cc, zz, xl = uu % 2, (uu // 2) % NZ, uu // (2 * NZ)
                    for k in range(2):
                        py[cc, g, 2 * yy + k, xl * NZ + zz] = go[i * 32 : i * 32 + 32, k * 128 : k * 128 + 128]

            return run

        z0 = dot(nb[...], wh[:, 0:512], NN)
        grad_h = dot(dm[...], wo[...], NN)
        beside(attention(z0, grad_h[:, 0:128], 0), [z_rows(i) for i in range(8)])
        middle()
        first = [f for j in range(4) for f in out_of(0, j)]
        beside(attention(z_s[...], grad_h[:, 128:256], 1), first)
        for j in range(4):
            both(j)()
            for f in out_of(1, j):
                f()

    def rows_out():
        for i in range(HIST):
            rows = pl.ds(i * SEQ, SEQ)
            dni, nfi = dn[rows, :], nf[rows, :]
            branch = (
                dni - jnp.mean(dni, axis=1, keepdims=True) - nfi * jnp.mean(dni * nfi, axis=1, keepdims=True)
            ) * rstd_s[rows, 0:1]
            out = (dm[rows, :].astype(F32) + branch).astype(BF16)
            for k in range(HEADS):
                dr[k, i] = out[:, k * 128 : k * 128 + 128]

    def head_parts(ref_of, g, hy):
        hx = lax.rem(g + hy, 2)
        return (
            ref_of(0).at[:, pl.ds(hy * 2, 2)],
            ref_of(1).at[pl.ds(hx * 2, 2), pl.ds((hy // 2) * NZ, NZ)],
            ref_of(2).at[hy],
        )

    def to_partner(g, hy):
        src = head_parts(lambda col: ps[col].at[1 - c, g], g, hy)
        dst = head_parts(lambda col: ts[col].at[g], g, hy)
        for col in range(3):
            s = (g * 3 + col) * 4 + hy
            remote(src[col], dst[col], par_send.at[s], par_recv.at[s], partner).start()

    def from_partner(part):
        g = part // 2
        for hy in (part % 2 * 2, part % 2 * 2 + 1):
            dst = head_parts(lambda col: ts[col].at[g], g, hy)
            for col in range(3):
                wait_bytes(dst[col], par_recv.at[(g * 3 + col) * 4 + hy])

    def add_parts(own_part, parts, count):
        step = min(count, 4 if own_part.shape[-1] == 128 else 2)

        @pl.loop(0, count // step)
        def _(i):
            rows = pl.ds(i * step, step)
            v = own_part[rows].astype(F32)
            for ref in parts:
                v = v + ref[rows].astype(F32)
            own_part[rows] = v.astype(BF16)

    def rz_half(ref, yy, half):
        return ref.at[pl.ds(yy * 4 + half * 2, 2)]

    def rs_sem(part, k, direction, half):
        return part * 16 + (direction * (NZ // 2) + k) * 2 + half

    def rs_add(part, off, half, from_ring):
        g, yy = part // 2, part % 2
        idx = lax.rem(z + off + NZ, NZ)
        parts = [rz_half(tz.at[g, idx], yy, half)]
        for k, direction in from_ring:
            s = rs_sem(part, k, direction, half)
            wait_bytes(rz.at[s], rs_recv.at[s])
            parts.append(rz.at[s])
        add_parts(rz_half(pz.at[c, g, idx], yy, half), parts, 2)

    def rs_step(part, k):
        g, yy = part // 2, part % 2
        for half in (0, 1):
            for direction in (0, 1):
                if k == 0 and half != direction:
                    continue
                off = NZ // 2 - k if direction == 0 else k - NZ // 2
                rs_add(part, off, half, ((k - 1, direction),) if k > 1 or (k == 1 and half == direction) else ())
                s = rs_sem(part, k, direction, half)
                remote(
                    rz_half(pz.at[c, g, lax.rem(z + off + NZ, NZ)], yy, half), rz.at[s],
                    rs_send.at[s], rs_recv.at[s], z_device(1 - 2 * direction),
                ).start()

    def send_x(part):
        g, yy = part // 2, part % 2
        sub = pl.ds(yy * NZ, NZ)
        for i in (2, 1, 3):
            q, device = last_peer(1, i)
            add_parts(px.at[c, g, q, sub], [tx.at[g, q, sub]], NZ)
            remote(
                px.at[c, g, q, sub], rx.at[g, x, sub], rl_send.at[part], rl_recv.at[part * 4 + x], device
            ).start()

    def send_y(g):
        for i in (2, 1, 3):
            q, device = last_peer(2, i)
            add_parts(py.at[c, g, q], [ty.at[g, q]], 16)
            remote(
                py.at[c, g, q], ry.at[g, y], rl_send.at[4 + g], rl_recv.at[16 + g * 4 + y], device
            ).start()

    def take_x(part):
        g, yy = part // 2, part % 2
        sub = pl.ds(yy * NZ, NZ)
        parts = [tx.at[g, x, sub]]
        for i in (1, 3, 2):
            q = x_peer(i)
            wait_bytes(rx.at[g, q, sub], rl_recv.at[part * 4 + q])
            parts.append(rx.at[g, q, sub])
        add_parts(px.at[c, g, x, sub], parts, NZ)
        for i in range(1, NY):
            q = y_peer(i)
            device = device_of(x, q, z, c)

            @pl.when((lax.rem(q + x_hi, 2) == g) & (q // 2 == yy))
            def _():
                remote(px.at[c, g, x, sub], s1x.at[y], o1_send.at[0], o1_recv.at[0], device).start()

    def take_y(g):
        parts = [ty.at[g, y]]
        for i in (1, 3, 2):
            q = y_peer(i)
            wait_bytes(ry.at[g, q], rl_recv.at[16 + g * 4 + q])
            parts.append(ry.at[g, q])
        add_parts(py.at[c, g, y], parts, 16)
        for i in range(1, NX):
            q = x_peer(i)
            device = device_of(q, y, z, c)

            @pl.when(lax.rem(y + q // 2, 2) == g)
            def _():
                remote(
                    py.at[c, g, y, pl.ds(lax.rem(q, 2) * NZ, NZ)], s1y.at[x], o1_send.at[1], o1_recv.at[1], device
                ).start()

    def take_z(part):
        g, yy = part // 2, part % 2
        for half in (0, 1):
            rs_add(part, 0, half, tuple((NZ // 2 - 1, d) for d in (0, 1)))
        for i in range(1, NY):
            q = y_peer(i)
            device = device_of(x, q, z, c)

            @pl.when(q // 2 == yy)
            def _():
                remote(
                    pz.at[c, g, z, pl.ds(q * 2, 2)], s1z.at[g, y], o1z_send.at[g], o1z_recv.at[g], device
                ).start()

    ag_start_z(0)
    ag_start_z(1)
    ag_start_xy(0)
    send_rows(0)
    send_rows(1)
    ag_step(0, 0)
    wait_bytes(tabs.at[c, 1 - x_lo], tab_recv.at[1])
    remote(tabs.at[c], tabs.at[c], tab_send.at[2], tab_recv.at[2], partner).start()
    ag_step(1, 0)
    ag_start_xy(1)
    ag_step(0, 1)
    ag_step(1, 1)
    ag_step(0, 2)
    ag_step(1, 2)
    ag_take_xy(0)
    norm_rows()
    ag_step(0, 3)
    ag_step(1, 3)
    mask_rows()
    ag_done(0)

    @pl.loop(0, 2)
    def _(j):
        def middle():
            @pl.when(j == 0)
            def _():
                ag_take_xy(1)

            @pl.when(j == 1)
            def _():
                from_partner(0)
                rs_step(0, 0)
                send_x(0)

        pair(0, j, middle)
        to_partner(0, 2 * j)
        to_partner(0, 2 * j + 1)
        pl.when(j == 1)(lambda: rs_step(0, 1))

    ag_done(1)

    @pl.loop(0, 2)
    def _(j):
        def middle():
            @pl.when(j == 0)
            def _():
                rs_step(0, 2)
                from_partner(1)
                rs_step(1, 0)
                send_x(1)
                send_y(0)

            @pl.when(j == 1)
            def _():
                rs_step(1, 2)
                from_partner(2)
                rs_step(2, 0)
                send_x(2)
                take_z(0)
                take_x(0)

        pair(1, j, middle)
        to_partner(1, 2 * j)
        to_partner(1, 2 * j + 1)

        @pl.when(j == 0)
        def _():
            rs_step(0, 3)
            rs_step(1, 1)

        @pl.when(j == 1)
        def _():
            rs_step(1, 3)
            rs_step(2, 1)

    rows_out()
    for i in range(1, HEADS):
        q = lax.rem(t + i, HEADS)
        remote(dr.at[q], grad_x.at[pl.ds(t * HIST, HIST)], out_send, out_recv, (u, q)).start()
    pltpu.make_async_copy(dr.at[t], grad_x.at[pl.ds(t * HIST, HIST)], loc.at[6]).start()
    from_partner(3)
    rs_step(3, 0)
    send_x(3)
    send_y(1)
    rs_step(2, 2)
    take_z(1)
    take_x(1)
    take_y(0)
    rs_step(3, 1)
    rs_step(2, 3)
    rs_step(3, 2)
    take_z(2)
    take_x(2)
    rs_step(3, 3)
    take_x(3)
    take_y(1)
    take_z(3)

    wait_bytes(s1x.at[pl.ds(0, NY - 1)], o1_recv.at[0])
    line_px = px.at[c, mine, x, pl.ds((y // 2) * NZ, NZ)]
    add_parts(line_px, [s1x.at[y_peer(i)] for i in range(1, NY)], NZ)
    for i in range(1, NZ):
        q = z_peer(i)
        remote(line_px.at[q], s2x.at[z], o2_send.at[1], o2_recv.at[1], device_of(x, y, q, c)).start()
    wait_bytes(s1y.at[pl.ds(0, NX - 1)], o1_recv.at[1])
    line_py = py.at[c, mine, y, pl.ds(x_lo * NZ, NZ)]
    add_parts(line_py, [s1y.at[x_peer(i)] for i in range(1, NX)], NZ)
    for i in range(1, NZ):
        q = z_peer(i)
        remote(line_py.at[q], s2y.at[z], o2_send.at[2], o2_recv.at[2], device_of(x, y, q, c)).start()
    for g in range(2):
        wait_bytes(s1z.at[g, pl.ds(0, NY - 1)], o1z_recv.at[g])
        add_parts(pz.at[c, g, z, pl.ds(y * 2, 2)], [s1z.at[g, y_peer(i)] for i in range(1, NY)], 2)
    for i in range(1, NX):
        q = x_peer(i)
        remote(
            pz.at[c, lax.rem(y + q // 2, 2), z, y * 2 + lax.rem(q, 2)], s2z.at[x], o2_send.at[0], o2_recv.at[0],
            device_of(q, y, z, c),
        ).start()

    wait_bytes(s2x.at[pl.ds(0, NZ - 1)], o2_recv.at[1])
    total = line_px[z].astype(F32)
    for i in range(1, NZ):
        total = total + s2x[z_peer(i)].astype(F32)
    grad_wi[:, pl.ds(384, 128)] = total
    wait_bytes(s2y.at[pl.ds(0, NZ - 1)], o2_recv.at[2])
    total = line_py[z].astype(F32)
    for i in range(1, NZ):
        total = total + s2y[z_peer(i)].astype(F32)
    grad_wo[...] = total
    wait_bytes(s2z.at[pl.ds(0, NX - 1)], o2_recv.at[0])
    total = pz[c, mine, z, y * 2 + x_lo].astype(F32)
    for i in range(1, NX):
        total = total + s2z[x_peer(i)].astype(F32)
    grad_wi[:, pl.ds(0, 384)] = total

    wait_bytes(gx.at[c, mine, x, pl.ds(0, NZ - 1)], st1_send.at[1])
    wait_bytes(gy.at[c, mine, y, pl.ds(0, NZ - 1)], st1_send.at[2])
    wait_bytes(gz.at[c, 0, z, pl.ds(0, NX - 1)], st1_send.at[0])
    wait_bytes(s1x.at[pl.ds(0, NY - 1)], st2_send.at[1])
    wait_bytes(s1y.at[pl.ds(0, NX - 1)], st2_send.at[2])
    for g in range(2):
        wait_bytes(gz.at[c, g, z, pl.ds(0, 6)], z2_send.at[g])
        wait_bytes(s1z.at[g, pl.ds(0, NY - 1)], o1z_send.at[g])
    wait_bytes(tabs.at[c, x_lo, pl.ds(0, NZ - 1)], tab_send.at[0])
    wait_bytes(tabs.at[c, x_lo], tab_send.at[1])
    wait_bytes(tabs.at[c], tab_send.at[2])
    wait_bytes(s1x.at[pl.ds(0, NY - 1)], o1_send.at[0])
    wait_bytes(s1y.at[pl.ds(0, NX - 1)], o1_send.at[1])
    wait_bytes(s2z.at[pl.ds(0, NX - 1)], o2_send.at[0])
    wait_bytes(s2x.at[pl.ds(0, NZ - 1)], o2_send.at[1])
    wait_bytes(s2y.at[pl.ds(0, NZ - 1)], o2_send.at[2])
    for k, ref in enumerate((xr, dr)):
        wait_bytes(ref.at[pl.ds(0, HEADS - 1)], a2a_send.at[k])
    for g in range(2):
        for col in range(3):
            wait_bytes(gs[col].at[c, g], fw_send.at[g * 3 + col])
            for hy in range(NY):
                dst = head_parts(lambda k: ts[k].at[g], g, hy)
                wait_bytes(dst[col], par_send.at[(g * 3 + col) * 4 + hy])
        for col in (1, 2):
            wait_bytes(rings[col].at[g, pl.ds(0, 3)], last_send.at[g * 2 + col - 1])
        for half in (0, 1):
            for direction in (0, 1):
                for k in range(NZ // 2):
                    s = ring_sem(g, k, direction, half)
                    if half == direction or k < NZ // 2 - 1:
                        wait_bytes(block(g, 0, half), ag_send.at[s])
                    if half == direction or k > 0:
                        for part in (2 * g, 2 * g + 1):
                            s = rs_sem(part, k, direction, half)
                            wait_bytes(rz.at[s], rs_send.at[s])
        wait_bytes(ry.at[g, pl.ds(0, 3)], rl_send.at[4 + g])
        for part in (2 * g, 2 * g + 1):
            wait_bytes(rx.at[g, pl.ds(0, 3), pl.ds(0, NZ)], rl_send.at[part])
    pltpu.make_async_copy(dr.at[t], grad_x.at[pl.ds(t * HIST, HIST)], loc.at[6]).wait()
    wait_bytes(dr.at[pl.ds(0, HEADS - 1)], out_send)
    wait_bytes(dr.at[pl.ds(0, HEADS - 1)], out_recv)


def hand_out(a, b, c, out_a, out_b, out_c):
    out_a[...] = a[...]
    out_b[...] = b[...]
    out_c[...] = c[...]


def local(events, cotangent, w_in, w_out, slot_source, slot_length):
    tab = jnp.pad(jnp.stack([slot_source, slot_length]), ((0, 6), (0, 96)))
    any_ = pl.BlockSpec(memory_space=pl.ANY)
    vmem = pl.BlockSpec(memory_space=pltpu.VMEM)
    shape = jax.ShapeDtypeStruct
    dma = pltpu.SemaphoreType.DMA
    both = [pltpu.VMEM((2, 2, n, m, 32, w), BF16) for _, n, m, w in COLOURS]
    theirs = [pltpu.VMEM((2, n, m, 32, w), BF16) for _, n, m, w in COLOURS]
    rings = [pltpu.VMEM((64, 2, 32, 384), BF16)] + [pltpu.VMEM((2, n, m, 32, w), BF16) for _, n, m, w in COLOURS[1:]]
    lines = [
        pltpu.VMEM((2, NY, 2, 32, 384), BF16),
        pltpu.VMEM((NY, NZ, 32, 128), BF16),
        pltpu.VMEM((NX, NZ, 32, 128), BF16),
        pltpu.VMEM((NX, 32, 384), BF16),
        pltpu.VMEM((NZ, 32, 128), BF16),
        pltpu.VMEM((NZ, 32, 128), BF16),
    ]
    work = [
        pltpu.VMEM((HEADS, HIST, SEQ, 128), BF16),
        pltpu.VMEM((HEADS, HIST, SEQ, 128), BF16),
        pltpu.VMEM((2, 2, NZ, 8, 128), jnp.int32),
        pltpu.VMEM((ROWS, D), F32),
        pltpu.VMEM((ROWS, D), BF16),
        pltpu.VMEM((D, ROWS), BF16),
        pltpu.VMEM((ROWS, D), BF16),
        pltpu.VMEM((D, ROWS), BF16),
        pltpu.VMEM((ROWS, 128), F32),
        pltpu.VMEM((ROWS, D), F32),
        pltpu.VMEM((D, 1024), BF16),
        pltpu.VMEM((D, 256), BF16),
        pltpu.VMEM((ROWS, 1024), BF16),
        pltpu.VMEM((ROWS, 256), BF16),
        pltpu.VMEM((ROWS, 512), F32),
    ]
    sems = [
        dma((7,)), dma((3,)), dma((3,)), dma((3,)), dma((2,)), dma((2,)), dma((NY,)), dma((NX,)),
        dma((32,)), dma((32,)), dma((6,)), dma((6,)), dma((2,)), dma((2,)), dma((3,)), dma((3,)),
        dma((24,)), dma((24,)), dma((64,)), dma((64,)), dma((4,)), dma((16,)), dma((6,)), dma((24,)),
        dma((2,)), dma((2,)), dma((2,)), dma((2,)), dma((3,)), dma((3,)), dma, dma,
    ]
    found = pl.pallas_call(
        kernel,
        out_shape=(shape((32, SEQ, 128), BF16), shape((32, 512), F32), shape((32, 128), F32)),
        in_specs=[any_, any_, any_, any_, any_],
        out_specs=(any_, vmem, vmem),
        scratch_shapes=both + both + theirs + rings + lines + work + sems,
        compiler_params=pltpu.CompilerParams(
            has_side_effects=True, collective_id=0, vmem_limit_bytes=64 * 1024 * 1024 - 131072
        ),
        name="step",
    )(events, cotangent, w_in, w_out, tab)
    specs = [
        pl.BlockSpec((8, SEQ, 128), lambda i: (i, 0, 0)),
        pl.BlockSpec((8, 512), lambda i: (i, 0)),
        pl.BlockSpec((8, 128), lambda i: (i, 0)),
    ]
    return pl.pallas_call(
        hand_out,
        grid=(4,),
        out_shape=tuple(shape(f.shape, f.dtype) for f in found),
        in_specs=specs,
        out_specs=tuple(specs),
        name="hand_out",
    )(*found)


def solution(mesh):
    in_specs = (
        P("user", None, "tensor"),
        P("user", None, "tensor"),
        P("user", "tensor"),
        P("user", "tensor"),
        P("user"),
        P("user"),
    )
    out_specs = (P("user", None, "tensor"), P("user", "tensor"), P("user", "tensor"))
    return jax.shard_map(local, mesh=mesh, in_specs=in_specs, out_specs=out_specs, check_vma=False)
```
